512 devices in a mesh: date: 64 (over z_lo, y, core), az: 8 (over z_hi, x).
Axes of the slice: x: 4, y: 4, z: 16 (z_hi: 2, z_lo: 8; z = z_hi * 8 + z_lo), core: 2. Of those that a mesh axis runs over, the one named last changes fastest.
Arguments:
- images: float32 [2, 64, 1024, 128], P(None, 'date', 'az'), may hold values from -12 to 12
- shifts: int32 [64, 2], P('date'), may hold values from -4 to 4, as said below
- fractions: int32 [64, 2], P('date'), may hold values from 0 to 15
- exponents: float32 [64], replicated, may hold values from 0.2 to 0.8
Outputs:
- filtered: float32 [2, 64, 1024, 128], P(None, 'date', 'az')
The draws below stay inside these ranges and needn't reach their ends.
Inputs may be any that keep to these rules, and one draw needn't show every extreme that they name: `shifts`: in every draw some date has both offsets equal to 4 and another date has both equal to -4.
All inputs are finite; a program needn't handle non-finite values.
Results may differ from the reference program's by a relative error of at most 0.0027.
Values may be sent and summed in bfloat16 or wider, within the bound.
No kernel may reach another device: no remote copies, remote signals or barrier semaphores. Data moves between devices by JAX's collectives and lax.ppermute only.
A program may use at most 64 MiB of HBM per device.

```python
import math
from functools import partial
import jax
import jax.numpy as jnp
from jax import lax

DATES = 64
PATCH = 16
HALF_WIN = 8
WIN = 17
TAPS = 8
SHIFT = 4
FRAC = 16
REACH = 8
ITERS = 3
ROWS = 1024
COLS = 128


def draw_images(key, part):
    subkeys = jax.random.split(key, 3)
    full_shape = (2, DATES, ROWS, COLS)
    noise_part = jax.random.normal(subkeys[0], full_shape, jnp.float32)
    date_scale = jnp.exp(jax.random.uniform(subkeys[1], (1, DATES, 1, 1), jnp.float32, -0.7, 0.7))
    pixel_scale = jnp.exp(jax.random.uniform(subkeys[2], (1, 1, ROWS, COLS), jnp.float32, -0.7, 0.7))
    values = noise_part * date_scale * pixel_scale
    return jnp.clip(values, -12.0, 12.0)


def draw_shifts(key, part):
    first_key, second_key = jax.random.split(key)
    drawn_values = jax.random.randint(first_key, (DATES, 2), -SHIFT, SHIFT + 1, jnp.int32)
    ranking = jax.random.permutation(second_key, DATES)
    drawn_values = drawn_values.at[ranking[0]].set(SHIFT)
    drawn_values = drawn_values.at[ranking[1]].set(-SHIFT)
    return drawn_values


def plant(array, stream_key, low, top_value):
    spot = [jax.random.randint(jax.random.fold_in(stream_key, axis), (), 0, length) for axis, length in enumerate(array.shape)]
    main_axis = array.shape.index(max(array.shape))
    beside = spot[:main_axis] + [(spot[main_axis] + 1) % array.shape[main_axis]] + spot[main_axis + 1:]
    return array.at[tuple(spot)].set(low).at[tuple(beside)].set(top_value)


def setup_inputs(seed: int = 0) -> dict:
    streams_of = jax.random.split(jax.random.key(seed), 5)
    return {
        "images": draw_images(jax.random.fold_in(streams_of[4], 71), 0),
        "shifts": draw_shifts(jax.random.fold_in(streams_of[4], 71), 0),
        "fractions": plant(jax.random.randint(streams_of[2], (DATES, 2), 0, FRAC), jax.random.fold_in(streams_of[2], 1), 0, FRAC - 1).astype(jnp.int32),
        "exponents": jnp.clip(jax.random.uniform(streams_of[3], (DATES,), jnp.float32, 0.2, 0.8), 0.2, 0.8),
    }


EPS = 1e-05
DAMP = 1.0

def sinc_taps(fraction):
    offsets = jnp.arange(TAPS, dtype=jnp.float32) - (TAPS // 2 - 1)
    position = offsets - fraction.astype(jnp.float32) / FRAC
    window_weight = 0.5 + 0.5 * jnp.cos(2.0 * math.pi * position / TAPS)
    return jnp.sinc(position) * window_weight

def apply_taps(source, weights, displacement, axis_number, extent):
    opening = REACH + displacement - (TAPS // 2 - 1)
    window_part = lax.dynamic_slice_in_dim(source, opening, extent + TAPS - 1, axis_number)
    summed = weights[0] * lax.slice_in_dim(window_part, 0, extent, axis=axis_number)
    for tap_index in range(1, TAPS):
        summed = summed + weights[tap_index] * lax.slice_in_dim(window_part, tap_index, tap_index + extent, axis=axis_number)
    return summed

def resample_block(extended, shift_pair, fraction_pair, extent):
    padded = jnp.pad(extended, ((0, 0), (0, 0), (REACH, REACH)))
    by_rows = apply_taps(padded, sinc_taps(fraction_pair[0]), shift_pair[0], 1, extent)
    return apply_taps(by_rows, sinc_taps(fraction_pair[1]), shift_pair[1], 2, extended.shape[2])

def apply_matrix(matrix, vector):
    return jnp.einsum('pmn,pn->pm', matrix, vector, precision=lax.Precision.HIGHEST)

def power_link(moment):
    count_dates = moment.shape[-1] // 2
    real_part = moment[:, :count_dates, :count_dates] + moment[:, count_dates:, count_dates:]
    imag_part = moment[:, count_dates:, :count_dates] - moment[:, :count_dates, count_dates:]
    diagonal_power = jnp.diagonal(real_part, axis1=1, axis2=2)
    scaling = lax.rsqrt(diagonal_power / (WIN * WIN) + EPS)
    outer_scale = scaling[:, :, None] * scaling[:, None, :] / (WIN * WIN)
    gamma_real = real_part * outer_scale
    gamma_imag = imag_part * outer_scale
    vector_real = jnp.ones(diagonal_power.shape, jnp.float32)
    vector_imag = jnp.zeros(diagonal_power.shape, jnp.float32)
    for iteration in range(ITERS):
        new_real = apply_matrix(gamma_real, vector_real) - apply_matrix(gamma_imag, vector_imag) + DAMP * vector_real
        new_imag = apply_matrix(gamma_real, vector_imag) + apply_matrix(gamma_imag, vector_real) + DAMP * vector_imag
        inverse_norm = lax.rsqrt(lax.optimization_barrier(jnp.sum(new_real * new_real + new_imag * new_imag, axis=1, keepdims=True)) / count_dates + EPS)
        vector_real = new_real * inverse_norm
        vector_imag = new_imag * inverse_norm
    return (vector_real, vector_imag)

def outer_rows(row_values):
    return jnp.einsum('jk,jl->jkl', row_values, row_values)

def link_phases(samples):
    planes = jnp.concatenate([samples[0], samples[1]], axis=0).astype(jnp.float32)
    stacked = jnp.transpose(planes, (1, 2, 0))
    padded = jnp.pad(stacked, ((HALF_WIN, HALF_WIN), (HALF_WIN, HALF_WIN), (0, 0)))

    def add_row(row_number, running):
        return running + outer_rows(lax.dynamic_index_in_dim(padded, row_number, 0, keepdims=False))
    initial = jnp.zeros((padded.shape[1], padded.shape[2], padded.shape[2]), jnp.float32)
    running = lax.fori_loop(0, WIN - 1, add_row, initial)

    def row_step(running, row_number):
        running = running + outer_rows(lax.dynamic_index_in_dim(padded, row_number + WIN - 1, 0, keepdims=False))
        cumulative = jnp.cumsum(running, axis=0)
        cumulative = jnp.concatenate([jnp.zeros_like(running[:1]), cumulative], axis=0)
        moment = cumulative[WIN:WIN + COLS] - cumulative[:COLS]
        result = power_link(moment)
        running = running - outer_rows(lax.dynamic_index_in_dim(padded, row_number, 0, keepdims=False))
        return (running, result)
    unused, linked_pair = lax.scan(row_step, running, jnp.arange(ROWS, dtype=jnp.int32))
    return linked_pair

def dft_tables(table_size):
    positions = jnp.arange(table_size, dtype=jnp.int32)
    same_block = positions[:, None] // PATCH == positions[None, :] // PATCH
    phase_index = positions[:, None] % PATCH * (positions[None, :] % PATCH) % PATCH
    angles = 2.0 * math.pi * phase_index.astype(jnp.float32) / PATCH
    table_real = jnp.where(same_block, jnp.cos(angles), 0.0) / math.sqrt(PATCH)
    table_imag = jnp.where(same_block, -jnp.sin(angles), 0.0) / math.sqrt(PATCH)
    return (table_real, table_imag)

def row_product(matrix, source):
    source_shape = source.shape
    blocked = source.reshape(source_shape[:-2] + (source_shape[-2] // PATCH, PATCH, source_shape[-1]))
    result = jnp.einsum('ij,...bjc->...bic', matrix, blocked, precision=lax.Precision.HIGHEST)
    return result.reshape(source_shape)

def column_product(source, matrix):
    return jnp.einsum('...c,cd->...d', source, matrix, precision=lax.Precision.HIGHEST)

def transform(source_real, source_imag, rows_real, rows_imag, cols_real, cols_imag):
    inner_real = row_product(rows_real, source_real) - row_product(rows_imag, source_imag)
    inner_imag = row_product(rows_real, source_imag) + row_product(rows_imag, source_real)
    outer_real = column_product(inner_real, cols_real) - column_product(inner_imag, cols_imag)
    outer_imag = column_product(inner_real, cols_imag) + column_product(inner_imag, cols_real)
    return (outer_real, outer_imag)

def patch_filter(field_real, field_imag, exponent):
    rows_real, rows_imag = dft_tables(PATCH)
    cols_real, cols_imag = dft_tables(field_real.shape[-1])
    spectrum_real, spectrum_imag = transform(field_real, field_imag, rows_real, rows_imag, cols_real, cols_imag)
    weighting = jnp.exp(exponent * jnp.log1p(spectrum_real * spectrum_real + spectrum_imag * spectrum_imag))
    return transform(spectrum_real * weighting, spectrum_imag * weighting, rows_real, -rows_imag, cols_real, -cols_imag)

def reference(images, shifts, fractions, exponents):
    padded = jnp.pad(images, ((0, 0), (0, 0), (REACH, REACH), (0, 0)))
    resampled = jax.vmap(partial(resample_block, extent=ROWS), in_axes=(1, 0, 0), out_axes=1)(padded, shifts, fractions)
    samples = resampled.astype(jnp.bfloat16)
    linked_real, linked_imag = link_phases(samples)
    field_real = jnp.transpose(linked_real, (2, 0, 1))
    field_imag = jnp.transpose(linked_imag, (2, 0, 1))
    filtered_real, filtered_imag = patch_filter(field_real, field_imag, exponents[:, None, None])
    return jnp.stack([filtered_real, filtered_imag])
```

```python
import math

import jax
import jax.numpy as jnp
import numpy as np
from jax import lax
from jax.experimental import pallas as pl
from jax.experimental.pallas import tpu as pltpu
from jax.sharding import PartitionSpec as P

PATCH = 16
HALF_WIN = 8
WIN = 17
TAPS = 8
FRAC = 16
REACH = 8
ITERS = 3
EPS = 1e-05
DAMP = 1.0

TILE = 16
SPAN = TILE + 2 * HALF_WIN
HALO = REACH + HALF_WIN
LANES = 128
GROUPS = LANES // SPAN
AREA = float(WIN * WIN)
LIMIT = 24 * 1024 * 1024

VMEM = pltpu.VMEM
SMEM = pltpu.SMEM
F32 = jnp.float32
BF16 = jnp.bfloat16


def tap_table():
    fraction = np.arange(FRAC, dtype=np.float64)[:, None] / FRAC
    position = np.arange(TAPS, dtype=np.float64)[None, :] - (TAPS // 2 - 1) - fraction
    window = 0.5 + 0.5 * np.cos(2.0 * math.pi * position / TAPS)
    return (np.sinc(position) * window).astype(np.float32)


def patch_transform():
    place = np.arange(TILE * TILE)
    rows, cols = place // TILE, place % TILE
    phase = (rows[:, None] * rows[None, :] + cols[:, None] * cols[None, :]) % PATCH
    angle = 2.0 * math.pi * phase / PATCH
    parts = []
    for full in (np.cos(angle) / PATCH, -np.sin(angle) / PATCH):
        high = full.astype(jnp.bfloat16)
        low = (full - high.astype(np.float64)).astype(jnp.bfloat16)
        parts += [high, low]
    return np.stack(parts)


def iota(shape, dim):
    return lax.broadcasted_iota(jnp.int32, shape, dim)


def split(value):
    high = value.astype(BF16)
    return high, (value - high.astype(F32)).astype(BF16)


def dot(a, b):
    return jnp.dot(a, b, preferred_element_type=F32)


def resample_kernel(
    last_block, shift_ref, fraction_ref, table_ref, block_ref, own_ref, before_ref, after_ref,
    out_ref, extended, rolled,
):
    rows = own_ref.shape[2]
    kept = rows + 2 * HALF_WIN
    shape = (kept, LANES)
    row_shift, col_shift = shift_ref[0, 0], shift_ref[0, 1]
    row_taps = [table_ref[fraction_ref[0, 0], tap] for tap in range(TAPS)]
    col_taps = [table_ref[fraction_ref[0, 1], tap] for tap in range(TAPS)]
    block = block_ref[0]
    row_at = iota(shape, 0)
    inside = jnp.logical_and(
        jnp.logical_or(block > 0, row_at >= HALF_WIN),
        jnp.logical_or(block < last_block, row_at < rows + HALF_WIN),
    )
    source = iota(shape, 1) + (col_shift - (TAPS // 2 - 1))
    turn = TAPS // 2 - 1 + LANES - col_shift
    for plane in range(2):
        extended[plane, 0:HALO] = before_ref[plane, 0]
        extended[plane, HALO : HALO + rows] = own_ref[plane, 0]
        extended[plane, HALO + rows : 2 * HALO + rows] = after_ref[plane, 0]
        opening = HALO - HALF_WIN - (TAPS // 2 - 1) + row_shift
        along = row_taps[0] * extended[plane, pl.ds(opening, kept), :]
        for tap in range(1, TAPS):
            along = along + row_taps[tap] * extended[plane, pl.ds(opening + tap, kept), :]
        total = None
        for tap in range(TAPS):
            moved = pltpu.roll(along, lax.rem(turn - tap, LANES), 1)
            at = source + tap
            moved = jnp.where(jnp.logical_and(at >= 0, at < LANES), moved, 0.0)
            total = col_taps[tap] * moved if tap == 0 else total + col_taps[tap] * moved
        total = jnp.where(inside, total, 0.0)
        for turn_step in range(LANES // TILE):
            rolled[turn_step, plane] = pltpu.roll(total, HALF_WIN + TILE * turn_step, 1)
    lane = iota((8, LANES), 1)
    group = lane // SPAN
    place = lane % SPAN
    tile_cols = LANES // TILE
    for tile_row in range(rows // TILE):
        for tile_col in range(tile_cols):
            planes = []
            for plane in range(2):
                tile = None
                for part in reversed(range(GROUPS)):
                    start = (2 * tile_row + part) * 8
                    piece = rolled[(2 * part - tile_col) % tile_cols, plane, start : start + 8, :]
                    tile = piece if tile is None else jnp.where(group == part, piece, tile)
                if tile_col == 0:
                    tile = jnp.where(place >= HALF_WIN, tile, 0.0)
                if tile_col == tile_cols - 1:
                    tile = jnp.where(place < HALF_WIN + TILE, tile, 0.0)
                planes.append(tile)
            both = jnp.concatenate(planes, axis=0)
            out_ref[tile_row * tile_cols + tile_col] = both.astype(BF16)


def resample(last_block, shifts, fractions, block, own, before, after):
    rows = own.shape[2]
    tiles = (rows // TILE) * (LANES // TILE)
    kept = rows + 2 * HALF_WIN
    smem = pl.BlockSpec(memory_space=SMEM)
    vmem = pl.BlockSpec(memory_space=VMEM)
    return pl.pallas_call(
        lambda *refs: resample_kernel(last_block, *refs),
        out_shape=jax.ShapeDtypeStruct((tiles, 2 * 8, LANES), BF16),
        in_specs=[smem] * 4 + [vmem] * 3,
        out_specs=vmem,
        scratch_shapes=[
            VMEM((2, rows + 2 * HALO, LANES), F32),
            VMEM((LANES // TILE, 2, kept, LANES), F32),
        ],
        compiler_params=pltpu.CompilerParams(vmem_limit_bytes=LIMIT),
        name="resample",
    )(shifts, fractions, tap_table(), block, own, before, after)


def link_kernel(
    tile_ref, exponent_ref, transform_ref, out_ref,
    loose, planes, pixels, mask, power, weights, vector,
):
    dates = tile_ref.shape[0]
    count = 2 * dates
    inner = TILE * TILE
    blocks = SPAN * SPAN // LANES
    loose[...] = tile_ref[...].astype(F32).reshape(loose.shape)
    at = iota((LANES, inner), 0)
    pixel = iota((LANES, inner), 1)
    col_lag = at % SPAN - pixel % TILE
    col_ok = jnp.logical_and(col_lag >= 0, col_lag < WIN)
    row_base = (at // SPAN) * 8 - pixel // TILE
    for b in range(blocks):
        here = slice(b * LANES, (b + 1) * LANES)
        real = loose[pl.ds(b, dates, stride=2 * blocks), :]
        imag = loose[pl.ds(blocks + b, dates, stride=2 * blocks), :]
        both = jnp.concatenate([real, imag], axis=0)
        planes[:, here] = both.astype(BF16)
        turned = both.T.astype(BF16)
        pixels[here, 0:count] = turned
        pixels[here, count : 2 * count] = turned
        high, low = split(real * real + imag * imag)
        power[0:dates, here] = high
        power[dates:count, here] = low
        row_lag = row_base + b
        ok = jnp.logical_and(col_ok, jnp.logical_and(row_lag >= 0, row_lag < WIN))
        mask[here, :] = jnp.where(ok, 1.0, 0.0)
    sums = dot(power[...], mask[...].astype(BF16))
    scaling = lax.rsqrt((sums[:dates] + sums[dates:]) / AREA + EPS)
    vector[0] = jnp.ones((dates, inner), F32)
    vector[1] = jnp.zeros((dates, inner), F32)

    def iterate(_, carry):
        real, imag = vector[0], vector[1]
        scaled_real, scaled_imag = scaling * real, scaling * imag
        rh, rl = split(scaled_real)
        ih, il = split(scaled_imag)
        weights[0:dates, 0:inner] = rh
        weights[0:dates, inner:] = ih
        weights[dates:count, 0:inner] = ih
        weights[dates:count, inner:] = -rh
        weights[count : count + dates, 0:inner] = rl
        weights[count : count + dates, inner:] = il
        weights[count + dates :, 0:inner] = il
        weights[count + dates :, inner:] = -rl
        total = jnp.zeros((count, 2 * inner), F32)
        step = 256
        for first in range(0, SPAN * SPAN, step):
            here = slice(first, first + step)
            inner_products = dot(pixels[here, :], weights[...])
            keep = mask[here, :]
            high, low = split(inner_products * jnp.concatenate([keep, keep], axis=1))
            total = total + dot(planes[:, here], high) + dot(planes[:, here], low)
        factor = scaling / AREA
        new_real = factor * (total[:dates, :inner] - total[dates:, inner:]) + DAMP * real
        new_imag = factor * (total[:dates, inner:] + total[dates:, :inner]) + DAMP * imag
        square = jnp.sum(new_real * new_real + new_imag * new_imag, axis=0, keepdims=True)
        inverse = lax.rsqrt(square / dates + EPS)
        vector[0] = new_real * inverse
        vector[1] = new_imag * inverse
        return carry

    lax.fori_loop(0, ITERS, iterate, 0)

    def transform(real, imag, sign):
        high, low = split(jnp.concatenate([real, imag], axis=0))
        stacked = jnp.concatenate([high, low], axis=0)
        cos = dot(stacked, transform_ref[0]) + dot(stacked, transform_ref[1])
        sin = dot(stacked, transform_ref[2]) + dot(stacked, transform_ref[3])
        cos = cos[:count] + cos[count:]
        sin = sign * (sin[:count] + sin[count:])
        return cos[:dates] - sin[dates:], sin[:dates] + cos[dates:]

    spectrum_real, spectrum_imag = transform(vector[0], vector[1], 1.0)
    square_shape = (dates, dates)
    own = jnp.where(iota(square_shape, 0) == iota(square_shape, 1), exponent_ref[...], 0.0)
    exponent = jnp.sum(own, axis=1, keepdims=True)
    size = spectrum_real * spectrum_real + spectrum_imag * spectrum_imag
    weighting = jnp.exp(exponent * jnp.log1p(size))
    real, imag = transform(spectrum_real * weighting, spectrum_imag * weighting, -1.0)
    out_ref[:, 0:inner] = real.astype(out_ref.dtype)
    out_ref[:, inner:] = imag.astype(out_ref.dtype)


def link(tile, exponents):
    dates = tile.shape[0]
    inner = TILE * TILE
    outer = SPAN * SPAN
    vmem = pl.BlockSpec(memory_space=VMEM)
    return pl.pallas_call(
        link_kernel,
        out_shape=jax.ShapeDtypeStruct((dates, 2 * inner), BF16),
        in_specs=[vmem] * 3,
        out_specs=vmem,
        scratch_shapes=[
            VMEM((2 * dates * outer // LANES, LANES), F32),
            VMEM((2 * dates, outer), BF16),
            VMEM((outer, 4 * dates), BF16),
            VMEM((outer, inner), F32),
            VMEM((2 * dates, outer), BF16),
            VMEM((4 * dates, 2 * inner), BF16),
            VMEM((2, dates, inner), F32),
        ],
        compiler_params=pltpu.CompilerParams(vmem_limit_bytes=LIMIT),
        name="link",
    )(tile, exponents.reshape(1, dates), patch_transform())


def unpack_kernel(tile_ref, out_ref):
    tile_cols = LANES // TILE
    shape = (8, LANES)
    sub = iota(shape, 0)
    column = iota(shape, 1) // TILE
    halves = TILE // 8
    for tile_row in range(tile_ref.shape[0] // tile_cols):
        for plane in range(2):
            for half in range(halves):
                first = (plane * halves + half) * LANES
                value = tile_ref[
                    tile_row * tile_cols : (tile_row + 1) * tile_cols, first : first + LANES
                ].astype(F32)
                for step in (1, 2, 4):
                    ahead = pltpu.roll(pltpu.roll(value, 8 - step, 0), TILE * step, 1)
                    behind = pltpu.roll(pltpu.roll(value, step, 0), LANES - TILE * step, 1)
                    sub_bit = jnp.bitwise_and(sub, step) != 0
                    col_bit = jnp.bitwise_and(column, step) != 0
                    swapped = jnp.where(sub_bit, behind, ahead)
                    value = jnp.where(sub_bit == col_bit, value, swapped)
                row = tile_row * TILE + half * 8
                out_ref[plane, 0, row : row + 8, :] = value


def unpack(tiles):
    rows = tiles.shape[0] * TILE * TILE // LANES
    vmem = pl.BlockSpec(memory_space=VMEM)
    return pl.pallas_call(
        unpack_kernel,
        out_shape=jax.ShapeDtypeStruct((2, 1, rows, LANES), F32),
        in_specs=[vmem],
        out_specs=vmem,
        compiler_params=pltpu.CompilerParams(vmem_limit_bytes=LIMIT),
        name="unpack",
    )(tiles)


def local(images, shifts, fractions, exponents):
    rows = images.shape[2]
    blocks = lax.axis_size("az")
    up = [(i, i + 1) for i in range(blocks - 1)]
    down = [(j, i) for i, j in up]
    before = lax.ppermute(lax.slice_in_dim(images, rows - HALO, rows, axis=2), "az", up)
    after = lax.ppermute(lax.slice_in_dim(images, 0, HALO, axis=2), "az", down)
    block = lax.axis_index("az").astype(jnp.int32).reshape(1)
    packed = resample(blocks - 1, shifts, fractions, block, images, before, after)
    tile = lax.all_to_all(packed, "date", split_axis=0, concat_axis=0, tiled=True)
    filtered = link(tile, exponents)
    returned = lax.all_to_all(filtered, "date", split_axis=0, concat_axis=0, tiled=True)
    return unpack(returned)


def solution(mesh):
    return jax.shard_map(
        local,
        mesh=mesh,
        in_specs=(P(None, "date", "az", None), P("date", None), P("date", None), P()),
        out_specs=P(None, "date", "az", None),
        check_vma=False,
    )
```

```python
import math

import jax
import jax.numpy as jnp
import numpy as np
from jax import lax
from jax.experimental import pallas as pl
from jax.experimental.pallas import tpu as pltpu
from jax.sharding import PartitionSpec as P

PATCH = 16
HALF_WIN = 8
WIN = 17
TAPS = 8
FRAC = 16
REACH = 8
ITERS = 3
EPS = 1e-05
DAMP = 1.0

TILE = 16
SPAN = TILE + 2 * HALF_WIN
HALO = REACH + HALF_WIN
LANES = 128
GROUPS = LANES // SPAN
AREA = float(WIN * WIN)
LIMIT = 24 * 1024 * 1024

VMEM = pltpu.VMEM
SMEM = pltpu.SMEM
F32 = jnp.float32
BF16 = jnp.bfloat16


def tap_table():
    fraction = np.arange(FRAC, dtype=np.float64)[:, None] / FRAC
    position = np.arange(TAPS, dtype=np.float64)[None, :] - (TAPS // 2 - 1) - fraction
    window = 0.5 + 0.5 * np.cos(2.0 * math.pi * position / TAPS)
    return (np.sinc(position) * window).astype(np.float32)


def patch_transform():
    place = np.arange(TILE * TILE)
    rows, cols = place // TILE, place % TILE
    phase = (rows[:, None] * rows[None, :] + cols[:, None] * cols[None, :]) % PATCH
    angle = 2.0 * math.pi * phase / PATCH
    parts = []
    for full in (np.cos(angle) / PATCH, -np.sin(angle) / PATCH):
        high = full.astype(jnp.bfloat16)
        low = (full - high.astype(np.float64)).astype(jnp.bfloat16)
        parts += [high, low]
    return np.stack(parts)


def iota(shape, dim):
    return lax.broadcasted_iota(jnp.int32, shape, dim)


def split(value):
    high = value.astype(BF16)
    return high, (value - high.astype(F32)).astype(BF16)


def dot(a, b):
    return jnp.dot(a, b, preferred_element_type=F32)


def read_taps(shift_ref, fraction_ref, table_ref):
    row_taps = [table_ref[fraction_ref[0, 0], tap] for tap in range(TAPS)]
    col_taps = [table_ref[fraction_ref[0, 1], tap] for tap in range(TAPS)]
    return shift_ref[0, 0], shift_ref[0, 1], row_taps, col_taps


def filter_rows(source, opening, kept, taps):
    along = taps[0] * source(opening, kept)
    for tap in range(1, TAPS):
        along = along + taps[tap] * source(opening + tap, kept)
    return along


def filter_cols(along, shift, taps):
    at = iota(along.shape, 1) + (shift - (TAPS // 2 - 1))
    turn = TAPS // 2 - 1 + LANES - shift
    total = None
    for tap in range(TAPS):
        moved = pltpu.roll(along, lax.rem(turn - tap, LANES), 1)
        here = at + tap
        moved = jnp.where(jnp.logical_and(here >= 0, here < LANES), moved, 0.0)
        total = taps[tap] * moved if tap == 0 else total + taps[tap] * moved
    return total


def inner_kernel(
    shift_ref, fraction_ref, table_ref, own_ref, exponent_ref, rolled_ref, mask_ref, exponent_out_ref
):
    row_shift, col_shift, row_taps, col_taps = read_taps(shift_ref, fraction_ref, table_ref)
    kept = own_ref.shape[2] - 2 * HALF_WIN
    opening = HALF_WIN - (TAPS // 2 - 1) + row_shift
    for plane in range(2):
        along = filter_rows(
            lambda first, size: own_ref[plane, 0, pl.ds(first, size), :], opening, kept, row_taps
        )
        total = filter_cols(along, col_shift, col_taps)
        for turn in range(LANES // TILE):
            rolled_ref[turn, plane] = pltpu.roll(total, HALF_WIN + TILE * turn, 1)
    inner = TILE * TILE
    at = iota((LANES, inner), 0)
    pixel = iota((LANES, inner), 1)
    col_lag = at % SPAN - pixel % TILE
    col_ok = jnp.logical_and(col_lag >= 0, col_lag < WIN)
    row_base = (at // SPAN) * 8 - pixel // TILE
    for b in range(SPAN * SPAN // LANES):
        row_lag = row_base + b
        ok = jnp.logical_and(col_ok, jnp.logical_and(row_lag >= 0, row_lag < WIN))
        mask_ref[b * LANES : (b + 1) * LANES, :] = jnp.where(ok, 1.0, 0.0).astype(BF16)
    exponent_out_ref[...] = exponent_ref[...]


def inner_resample(shifts, fractions, own, exponents):
    rows = own.shape[2]
    kept = rows - 2 * HALF_WIN
    smem = pl.BlockSpec(memory_space=SMEM)
    vmem = pl.BlockSpec(memory_space=VMEM)
    return pl.pallas_call(
        inner_kernel,
        out_shape=(
            jax.ShapeDtypeStruct((LANES // TILE, 2, kept, LANES), F32),
            jax.ShapeDtypeStruct((SPAN * SPAN, TILE * TILE), BF16),
            jax.ShapeDtypeStruct(exponents.shape, F32),
        ),
        in_specs=[smem] * 3 + [vmem] * 2,
        out_specs=(vmem,) * 3,
        compiler_params=pltpu.CompilerParams(vmem_limit_bytes=LIMIT),
        cost_estimate=pl.CostEstimate(flops=2000000, bytes_accessed=2000000, transcendentals=0),
        name="inner_resample",
    )(shifts, fractions, tap_table(), own, exponents)


def edge_kernel(
    last_block, shift_ref, fraction_ref, table_ref, block_ref, own_ref, even_ref, odd_ref, rolled_ref,
    out_ref, extended, edges,
):
    rows = own_ref.shape[2]
    row_shift, col_shift, row_taps, col_taps = read_taps(shift_ref, fraction_ref, table_ref)
    block = block_ref[0]
    is_even = lax.rem(block, 2) == 0
    tile_cols = LANES // TILE
    opening = HALO - HALF_WIN - (TAPS // 2 - 1) + row_shift
    for side in range(2):
        row_at = iota((HALO, LANES), 0)
        if side == 0:
            inside = jnp.logical_or(block > 0, row_at >= HALF_WIN)
        else:
            inside = jnp.logical_or(block < last_block, row_at < HALF_WIN)
        for plane in range(2):
            from_even = even_ref[plane, 0]
            from_odd = odd_ref[plane, 0]
            if side == 0:
                extended[0:HALO] = jnp.where(is_even, from_odd, from_even)
                extended[HALO : 2 * HALO] = own_ref[plane, 0, 0:HALO]
            else:
                extended[0:HALO] = own_ref[plane, 0, rows - HALO : rows]
                extended[HALO : 2 * HALO] = jnp.where(is_even, from_even, from_odd)
            along = filter_rows(
                lambda first, size: extended[pl.ds(first, size), :], opening, HALO, row_taps
            )
            total = jnp.where(inside, filter_cols(along, col_shift, col_taps), 0.0)
            for turn in range(tile_cols):
                edges[turn, plane, side * HALO : (side + 1) * HALO] = pltpu.roll(
                    total, HALF_WIN + TILE * turn, 1
                )

    def piece(turn, plane, step):
        last = rows // 8 + 2
        if step < 2:
            return edges[turn, plane, step * 8 : step * 8 + 8, :]
        if step >= last - 2:
            start = HALO + (step - last + 2) * 8
            return edges[turn, plane, start : start + 8, :]
        return rolled_ref[turn, plane, (step - 2) * 8 : (step - 1) * 8, :]

    lane = iota((8, LANES), 1)
    group = lane // SPAN
    place = lane % SPAN
    for tile_row in range(rows // TILE):
        for tile_col in range(tile_cols):
            planes = []
            for plane in range(2):
                tile = None
                for part in reversed(range(GROUPS)):
                    this = piece((2 * part - tile_col) % tile_cols, plane, 2 * tile_row + part)
                    tile = this if tile is None else jnp.where(group == part, this, tile)
                if tile_col == 0:
                    tile = jnp.where(place >= HALF_WIN, tile, 0.0)
                if tile_col == tile_cols - 1:
                    tile = jnp.where(place < HALF_WIN + TILE, tile, 0.0)
                planes.append(tile)
            both = jnp.concatenate(planes, axis=0)
            out_ref[tile_row * tile_cols + tile_col] = both.astype(BF16)


def edge_resample(last_block, shifts, fractions, block, own, even, odd, rolled):
    rows = own.shape[2]
    tiles = (rows // TILE) * (LANES // TILE)
    smem = pl.BlockSpec(memory_space=SMEM)
    vmem = pl.BlockSpec(memory_space=VMEM)
    return pl.pallas_call(
        lambda *refs: edge_kernel(last_block, *refs),
        out_shape=jax.ShapeDtypeStruct((tiles, 2 * 8, LANES), BF16),
        in_specs=[smem] * 4 + [vmem] * 4,
        out_specs=vmem,
        scratch_shapes=[
            VMEM((2 * HALO, LANES), F32),
            VMEM((LANES // TILE, 2, 2 * HALO, LANES), F32),
        ],
        compiler_params=pltpu.CompilerParams(vmem_limit_bytes=LIMIT),
        name="edge_resample",
    )(shifts, fractions, tap_table(), block, own, even, odd, rolled)


def link_kernel(
    tile_ref, exponent_ref, transform_ref, mask, out_ref,
    loose, planes, pixels, power, weights, vector,
):
    dates = tile_ref.shape[0]
    count = 2 * dates
    inner = TILE * TILE
    blocks = SPAN * SPAN // LANES
    loose[...] = tile_ref[...].astype(F32).reshape(loose.shape)
    for b in range(blocks):
        here = slice(b * LANES, (b + 1) * LANES)
        real = loose[pl.ds(b, dates, stride=2 * blocks), :]
        imag = loose[pl.ds(blocks + b, dates, stride=2 * blocks), :]
        both = jnp.concatenate([real, imag], axis=0)
        planes[:, here] = both.astype(BF16)
        turned = both.T.astype(BF16)
        pixels[here, 0:count] = turned
        pixels[here, count : 2 * count] = turned
        high, low = split(real * real + imag * imag)
        power[0:dates, here] = high
        power[dates:count, here] = low
    sums = dot(power[...], mask[...])
    scaling = lax.rsqrt((sums[:dates] + sums[dates:]) / AREA + EPS)
    vector[0] = jnp.ones((dates, inner), F32)
    vector[1] = jnp.zeros((dates, inner), F32)

    def iterate(_, carry):
        real, imag = vector[0], vector[1]
        scaled_real, scaled_imag = scaling * real, scaling * imag
        rh, rl = split(scaled_real)
        ih, il = split(scaled_imag)
        weights[0:dates, 0:inner] = rh
        weights[0:dates, inner:] = ih
        weights[dates:count, 0:inner] = ih
        weights[dates:count, inner:] = -rh
        weights[count : count + dates, 0:inner] = rl
        weights[count : count + dates, inner:] = il
        weights[count + dates :, 0:inner] = il
        weights[count + dates :, inner:] = -rl
        total = jnp.zeros((count, 2 * inner), F32)
        step = 256
        for first in range(0, SPAN * SPAN, step):
            here = slice(first, first + step)
            inner_products = dot(pixels[here, :], weights[...])
            keep = mask[here, :].astype(F32)
            high, low = split(inner_products * jnp.concatenate([keep, keep], axis=1))
            total = total + dot(planes[:, here], high) + dot(planes[:, here], low)
        factor = scaling / AREA
        new_real = factor * (total[:dates, :inner] - total[dates:, inner:]) + DAMP * real
        new_imag = factor * (total[:dates, inner:] + total[dates:, :inner]) + DAMP * imag
        square = jnp.sum(new_real * new_real + new_imag * new_imag, axis=0, keepdims=True)
        inverse = lax.rsqrt(square / dates + EPS)
        vector[0] = new_real * inverse
        vector[1] = new_imag * inverse
        return carry

    lax.fori_loop(0, ITERS, iterate, 0)

    def transform(real, imag, sign):
        high, low = split(jnp.concatenate([real, imag], axis=0))
        stacked = jnp.concatenate([high, low], axis=0)
        cos = dot(stacked, transform_ref[0]) + dot(stacked, transform_ref[1])
        sin = dot(stacked, transform_ref[2]) + dot(stacked, transform_ref[3])
        cos = cos[:count] + cos[count:]
        sin = sign * (sin[:count] + sin[count:])
        return cos[:dates] - sin[dates:], sin[:dates] + cos[dates:]

    spectrum_real, spectrum_imag = transform(vector[0], vector[1], 1.0)
    square_shape = (dates, dates)
    own = jnp.where(iota(square_shape, 0) == iota(square_shape, 1), exponent_ref[...], 0.0)
    exponent = jnp.sum(own, axis=1, keepdims=True)
    size = spectrum_real * spectrum_real + spectrum_imag * spectrum_imag
    weighting = jnp.exp(exponent * jnp.log1p(size))
    real, imag = transform(spectrum_real * weighting, spectrum_imag * weighting, -1.0)
    out_ref[:, 0:inner] = real.astype(out_ref.dtype)
    out_ref[:, inner:] = imag.astype(out_ref.dtype)


def link(tile, exponents, mask):
    dates = tile.shape[0]
    inner = TILE * TILE
    outer = SPAN * SPAN
    vmem = pl.BlockSpec(memory_space=VMEM)
    return pl.pallas_call(
        link_kernel,
        out_shape=jax.ShapeDtypeStruct((dates, 2 * inner), BF16),
        in_specs=[vmem] * 4,
        out_specs=vmem,
        scratch_shapes=[
            VMEM((2 * dates * outer // LANES, LANES), F32),
            VMEM((2 * dates, outer), BF16),
            VMEM((outer, 4 * dates), BF16),
            VMEM((2 * dates, outer), BF16),
            VMEM((4 * dates, 2 * inner), BF16),
            VMEM((2, dates, inner), F32),
        ],
        compiler_params=pltpu.CompilerParams(vmem_limit_bytes=LIMIT),
        name="link",
    )(tile, exponents, patch_transform(), mask)


def unpack_kernel(tile_ref, out_ref):
    tile_cols = LANES // TILE
    shape = (8, LANES)
    sub = iota(shape, 0)
    column = iota(shape, 1) // TILE
    halves = TILE // 8
    for tile_row in range(tile_ref.shape[0] // tile_cols):
        for plane in range(2):
            for half in range(halves):
                first = (plane * halves + half) * LANES
                value = tile_ref[
                    tile_row * tile_cols : (tile_row + 1) * tile_cols, first : first + LANES
                ].astype(F32)
                for step in (1, 2, 4):
                    ahead = pltpu.roll(pltpu.roll(value, 8 - step, 0), TILE * step, 1)
                    behind = pltpu.roll(pltpu.roll(value, step, 0), LANES - TILE * step, 1)
                    sub_bit = jnp.bitwise_and(sub, step) != 0
                    col_bit = jnp.bitwise_and(column, step) != 0
                    swapped = jnp.where(sub_bit, behind, ahead)
                    value = jnp.where(sub_bit == col_bit, value, swapped)
                row = tile_row * TILE + half * 8
                out_ref[plane, 0, row : row + 8, :] = value


def unpack(tiles):
    rows = tiles.shape[0] * TILE * TILE // LANES
    vmem = pl.BlockSpec(memory_space=VMEM)
    return pl.pallas_call(
        unpack_kernel,
        out_shape=jax.ShapeDtypeStruct((2, 1, rows, LANES), F32),
        in_specs=[vmem],
        out_specs=vmem,
        compiler_params=pltpu.CompilerParams(vmem_limit_bytes=LIMIT),
        name="unpack",
    )(tiles)


def both_ways(boundaries):
    return [(k, k + 1) for k in boundaries] + [(k + 1, k) for k in boundaries]


def local(images, shifts, fractions, exponents):
    rows = images.shape[2]
    blocks = lax.axis_size("az")
    block = lax.axis_index("az").astype(jnp.int32)
    first = lax.slice_in_dim(images, 0, HALO, axis=2)
    last = lax.slice_in_dim(images, rows - HALO, rows, axis=2)
    is_even = lax.rem(block, 2) == 0
    to_odd = jnp.where(is_even, first, last)
    to_even = jnp.where(is_even, last, first)
    odd = lax.ppermute(to_odd, "az", both_ways(range(1, blocks - 1, 2)))
    even = lax.ppermute(to_even, "az", both_ways(range(0, blocks - 1, 2)))
    rolled, mask, exponent_row = inner_resample(
        shifts, fractions, images, exponents.reshape(1, exponents.shape[0])
    )
    packed = edge_resample(
        blocks - 1, shifts, fractions, block.reshape(1), images, even, odd, rolled
    )
    tile = lax.all_to_all(packed, "date", split_axis=0, concat_axis=0, tiled=True)
    filtered = link(tile, exponent_row, mask)
    filtered = filtered.reshape(filtered.shape[0], -1, LANES)
    returned = lax.all_to_all(filtered, "date", split_axis=0, concat_axis=0, tiled=True)
    return unpack(returned.reshape(returned.shape[0], -1))


def solution(mesh):
    return jax.shard_map(
        local,
        mesh=mesh,
        in_specs=(P(None, "date", "az", None), P("date", None), P("date", None), P()),
        out_specs=P(None, "date", "az", None),
        check_vma=False,
    )
```

```python
import math

import jax
import jax.numpy as jnp
import numpy as np
from jax import lax
from jax.experimental import pallas as pl
from jax.experimental.pallas import tpu as pltpu
from jax.sharding import PartitionSpec as P

PATCH = 16
HALF_WIN = 8
WIN = 17
TAPS = 8
FRAC = 16
REACH = 8
ITERS = 3
EPS = 1e-05
DAMP = 1.0

TILE = 16
SPAN = TILE + 2 * HALF_WIN
HALO = REACH + HALF_WIN
LANES = 128
GROUPS = LANES // SPAN
HALF_TILE = TILE * TILE // 2
HALF_SPAN = (TILE // 2 + 2 * HALF_WIN) * SPAN
AREA = float(WIN * WIN)
LIMIT = 24 * 1024 * 1024

VMEM = pltpu.VMEM
SMEM = pltpu.SMEM
F32 = jnp.float32
BF16 = jnp.bfloat16


def tap_table():
    fraction = np.arange(FRAC, dtype=np.float64)[:, None] / FRAC
    position = np.arange(TAPS, dtype=np.float64)[None, :] - (TAPS // 2 - 1) - fraction
    window = 0.5 + 0.5 * np.cos(2.0 * math.pi * position / TAPS)
    return (np.sinc(position) * window).astype(np.float32)


def patch_transform():
    place = np.arange(TILE * TILE)
    rows, cols = place // TILE, place % TILE
    phase = (rows[:, None] * rows[None, :] + cols[:, None] * cols[None, :]) % PATCH
    angle = 2.0 * math.pi * phase / PATCH
    parts = []
    for full in (np.cos(angle) / PATCH, -np.sin(angle) / PATCH):
        high = full.astype(jnp.bfloat16)
        low = (full - high.astype(np.float64)).astype(jnp.bfloat16)
        parts += [high, low]
    return np.stack(parts)


def iota(shape, dim):
    return lax.broadcasted_iota(jnp.int32, shape, dim)


def split(value):
    high = value.astype(BF16)
    return high, (value - high.astype(F32)).astype(BF16)


def dot(a, b):
    return jnp.dot(a, b, preferred_element_type=F32)


def read_taps(shift_ref, fraction_ref, table_ref):
    row_taps = [table_ref[fraction_ref[0, 0], tap] for tap in range(TAPS)]
    col_taps = [table_ref[fraction_ref[0, 1], tap] for tap in range(TAPS)]
    return shift_ref[0, 0], shift_ref[0, 1], row_taps, col_taps


def filter_rows(source, opening, kept, taps):
    along = taps[0] * source(opening, kept)
    for tap in range(1, TAPS):
        along = along + taps[tap] * source(opening + tap, kept)
    return along


def filter_cols(along, shift, taps):
    at = iota(along.shape, 1) + (shift - (TAPS // 2 - 1))
    turn = TAPS // 2 - 1 + LANES - shift
    total = None
    for tap in range(TAPS):
        moved = pltpu.roll(along, lax.rem(turn - tap, LANES), 1)
        here = at + tap
        moved = jnp.where(jnp.logical_and(here >= 0, here < LANES), moved, 0.0)
        total = taps[tap] * moved if tap == 0 else total + taps[tap] * moved
    return total


def pack_tile(strip_piece, tile_col):
    lane = iota((8, LANES), 1)
    group = lane // SPAN
    place = lane % SPAN
    planes = []
    for plane in range(2):
        tile = None
        for part in reversed(range(GROUPS)):
            this = strip_piece((2 * part - tile_col) % (LANES // TILE), plane, part)
            tile = this if tile is None else jnp.where(group == part, this, tile)
        if tile_col == 0:
            tile = jnp.where(place >= HALF_WIN, tile, 0.0)
        if tile_col == LANES // TILE - 1:
            tile = jnp.where(place < HALF_WIN + TILE, tile, 0.0)
        planes.append(tile)
    return jnp.concatenate(planes, axis=0).astype(BF16)


def inner_kernel(
    shift_ref, fraction_ref, table_ref, own_ref, exponent_ref,
    packed_ref, near_ref, mask_ref, exponent_out_ref, step_ref, tap_ref, rolled,
):
    row_shift, col_shift, row_taps, col_taps = read_taps(shift_ref, fraction_ref, table_ref)
    rows = own_ref.shape[2]
    kept = rows - 2 * HALF_WIN
    opening = HALF_WIN - (TAPS // 2 - 1) + row_shift
    tile_cols = LANES // TILE
    for plane in range(2):
        along = filter_rows(
            lambda first, size: own_ref[plane, 0, pl.ds(first, size), :], opening, kept, row_taps
        )
        total = filter_cols(along, col_shift, col_taps)
        for turn in range(tile_cols):
            moved = pltpu.roll(total, HALF_WIN + TILE * turn, 1)
            rolled[turn, plane] = moved
            near_ref[0, turn, plane] = moved[0:HALO]
            near_ref[1, turn, plane] = moved[kept - HALO : kept]
    for tile_row in range(1, rows // TILE - 1):
        first = (tile_row - 1) * TILE
        for tile_col in range(tile_cols):
            packed_ref[tile_row * tile_cols + tile_col] = pack_tile(
                lambda turn, plane, part: rolled[
                    turn, plane, pl.ds(first + part, 8, stride=GROUPS), :
                ],
                tile_col,
            )
    shape = mask_ref.shape
    at = iota(shape, 0)
    pixel = iota(shape, 1)
    row_lag = at // SPAN - pixel // TILE
    col_lag = at % SPAN - pixel % TILE
    row_ok = jnp.logical_and(row_lag >= 0, row_lag < WIN)
    col_ok = jnp.logical_and(col_lag >= 0, col_lag < WIN)
    mask_ref[...] = jnp.where(jnp.logical_and(row_ok, col_ok), 1.0, 0.0).astype(BF16)
    exponent_out_ref[...] = exponent_ref[...]
    step_ref[0:1, :] = jnp.full((1, LANES), row_shift, jnp.int32)
    step_ref[1:2, :] = jnp.full((1, LANES), col_shift, jnp.int32)
    for tap in range(TAPS):
        tap_ref[tap : tap + 1, :] = jnp.full((1, LANES), row_taps[tap], F32)
        tap_ref[TAPS + tap : TAPS + tap + 1, :] = jnp.full((1, LANES), col_taps[tap], F32)


def inner_resample(shifts, fractions, own, exponents):
    rows = own.shape[2]
    tiles = (rows // TILE) * (LANES // TILE)
    kept = rows - 2 * HALF_WIN
    smem = pl.BlockSpec(memory_space=SMEM)
    vmem = pl.BlockSpec(memory_space=VMEM)
    return pl.pallas_call(
        inner_kernel,
        out_shape=(
            jax.ShapeDtypeStruct((tiles, 2 * 8, LANES), BF16),
            jax.ShapeDtypeStruct((2, LANES // TILE, 2, HALO, LANES), F32),
            jax.ShapeDtypeStruct((HALF_SPAN, HALF_TILE), BF16),
            jax.ShapeDtypeStruct(exponents.shape, F32),
            jax.ShapeDtypeStruct((2, LANES), jnp.int32),
            jax.ShapeDtypeStruct((2 * TAPS, LANES), F32),
        ),
        in_specs=[smem] * 3 + [vmem] * 2,
        out_specs=(vmem,) * 6,
        scratch_shapes=[VMEM((LANES // TILE, 2, kept, LANES), F32)],
        compiler_params=pltpu.CompilerParams(vmem_limit_bytes=LIMIT),
        cost_estimate=pl.CostEstimate(flops=2000000, bytes_accessed=2000000, transcendentals=0),
        name="inner_resample",
    )(shifts, fractions, tap_table(), own, exponents)


def az_block():
    return lax.axis_index("az").astype(jnp.int32)


def edge_kernel(
    last_block, step_ref, tap_ref, own_ref, even_ref, odd_ref, packed_in_ref, near_ref,
    packed_ref, strip, extended,
):
    rows = own_ref.shape[2]
    row_shift, col_shift = jnp.max(step_ref[0:1, :]), jnp.max(step_ref[1:2, :])
    row_taps = [tap_ref[tap : tap + 1, :] for tap in range(TAPS)]
    col_taps = [tap_ref[TAPS + tap : TAPS + tap + 1, :] for tap in range(TAPS)]
    block = az_block()
    is_even = lax.rem(block, 2) == 0
    tile_cols = LANES // TILE
    tile_rows = rows // TILE
    opening = HALO - HALF_WIN - (TAPS // 2 - 1) + row_shift
    packed_ref[tile_cols : (tile_rows - 1) * tile_cols] = packed_in_ref[
        tile_cols : (tile_rows - 1) * tile_cols
    ]
    for side in range(2):
        row_at = iota((HALO, LANES), 0)
        if side == 0:
            inside = jnp.logical_or(block > 0, row_at >= HALF_WIN)
        else:
            inside = jnp.logical_or(block < last_block, row_at < HALF_WIN)
        for plane in range(2):
            from_even = even_ref[plane, 0]
            from_odd = odd_ref[plane, 0]
            if side == 0:
                extended[side, plane, 0:HALO] = jnp.where(is_even, from_odd, from_even)
                extended[side, plane, HALO : 2 * HALO] = own_ref[plane, 0, 0:HALO]
            else:
                extended[side, plane, 0:HALO] = own_ref[plane, 0, rows - HALO : rows]
                extended[side, plane, HALO : 2 * HALO] = jnp.where(is_even, from_even, from_odd)
            along = filter_rows(
                lambda first, size: extended[side, plane, pl.ds(first, size), :],
                opening, HALO, row_taps,
            )
            total = jnp.where(inside, filter_cols(along, col_shift, col_taps), 0.0)
            for turn in range(tile_cols):
                strip[side, turn, plane, side * HALO : (side + 1) * HALO] = pltpu.roll(
                    total, HALF_WIN + TILE * turn, 1
                )
                strip[side, turn, plane, (1 - side) * HALO : (2 - side) * HALO] = near_ref[
                    side, turn, plane
                ]
        tile_row = side * (tile_rows - 1)
        for tile_col in range(tile_cols):
            packed_ref[tile_row * tile_cols + tile_col] = pack_tile(
                lambda turn, plane, part: strip[
                    side, turn, plane, pl.ds(part, 8, stride=GROUPS), :
                ],
                tile_col,
            )


def edge_resample(last_block, steps, taps, own, even, odd, packed, near):
    vmem = pl.BlockSpec(memory_space=VMEM)
    return pl.pallas_call(
        lambda *refs: edge_kernel(last_block, *refs),
        out_shape=jax.ShapeDtypeStruct(packed.shape, packed.dtype),
        in_specs=[vmem] * 7,
        out_specs=vmem,
        scratch_shapes=[
            VMEM((2, LANES // TILE, 2, 2 * HALO, LANES), F32),
            VMEM((2, 2, 2 * HALO, LANES), F32),
        ],
        compiler_params=pltpu.CompilerParams(vmem_limit_bytes=LIMIT),
        name="edge_resample",
    )(steps, taps, own, even, odd, packed, near)


def link_kernel(
    tile_ref, exponent_ref, transform_ref, mask, out_ref,
    loose, planes, pixels, power, vector,
):
    dates = tile_ref.shape[0]
    count = 2 * dates
    inner = TILE * TILE
    blocks = SPAN * SPAN // LANES
    loose[...] = tile_ref[...].astype(F32).reshape(loose.shape)
    for b in range(blocks):
        here = slice(b * LANES, (b + 1) * LANES)
        real = loose[pl.ds(b, dates, stride=2 * blocks), :]
        imag = loose[pl.ds(blocks + b, dates, stride=2 * blocks), :]
        both = jnp.concatenate([real, imag], axis=0)
        planes[:, here] = both.astype(BF16)
        turned = both.T.astype(BF16)
        pixels[here, 0:count] = turned
        pixels[here, count : 2 * count] = turned
        high, low = split(real * real + imag * imag)
        power[0:dates, here] = high
        power[dates:count, here] = low
    starts = [half * (SPAN * TILE // 2) for half in range(2)]
    keep = mask[...]
    sums = jnp.concatenate([dot(power[:, first : first + HALF_SPAN], keep) for first in starts], axis=1)
    scaling = lax.rsqrt((sums[:dates] + sums[dates:]) / AREA + EPS)
    vector[0] = jnp.ones((dates, inner), F32)
    vector[1] = jnp.zeros((dates, inner), F32)

    def iterate(_, carry):
        for half in range(2):
            cols = slice(half * HALF_TILE, (half + 1) * HALF_TILE)
            real, imag = vector[0, :, cols], vector[1, :, cols]
            scale = scaling[:, cols]
            rh, rl = split(scale * real)
            ih, il = split(scale * imag)
            top = [jnp.concatenate(pair, axis=1) for pair in ((rh, ih), (ih, -rh), (rl, il), (il, -rl))]
            weights = jnp.concatenate(top, axis=0)
            total = jnp.zeros((count, 2 * HALF_TILE), F32)
            step = 256
            for first in range(0, HALF_SPAN, step):
                here = slice(starts[half] + first, starts[half] + first + step)
                near = mask[first : first + step, :].astype(F32)
                products = dot(pixels[here, :], weights)
                kept = (products * jnp.concatenate([near, near], axis=1)).astype(BF16)
                total = total + dot(planes[:, here], kept)
            factor = scale / AREA
            left, right = slice(0, HALF_TILE), slice(HALF_TILE, 2 * HALF_TILE)
            new_real = factor * (total[:dates, left] - total[dates:, right]) + DAMP * real
            new_imag = factor * (total[:dates, right] + total[dates:, left]) + DAMP * imag
            square = jnp.sum(new_real * new_real + new_imag * new_imag, axis=0, keepdims=True)
            inverse = lax.rsqrt(square / dates + EPS)
            vector[0, :, cols] = new_real * inverse
            vector[1, :, cols] = new_imag * inverse
        return carry

    lax.fori_loop(0, ITERS, iterate, 0)

    def transform(real, imag, sign):
        high, low = split(jnp.concatenate([real, imag], axis=0))
        stacked = jnp.concatenate([high, low], axis=0)
        cos = dot(stacked, transform_ref[0]) + dot(stacked, transform_ref[1])
        sin = dot(stacked, transform_ref[2]) + dot(stacked, transform_ref[3])
        cos = cos[:count] + cos[count:]
        sin = sign * (sin[:count] + sin[count:])
        return cos[:dates] - sin[dates:], sin[:dates] + cos[dates:]

    spectrum_real, spectrum_imag = transform(vector[0], vector[1], 1.0)
    square_shape = (dates, dates)
    own = jnp.where(iota(square_shape, 0) == iota(square_shape, 1), exponent_ref[...], 0.0)
    exponent = jnp.sum(own, axis=1, keepdims=True)
    size = spectrum_real * spectrum_real + spectrum_imag * spectrum_imag
    weighting = jnp.exp(exponent * jnp.log1p(size))
    real, imag = transform(spectrum_real * weighting, spectrum_imag * weighting, -1.0)
    out_ref[:, 0:inner] = real.astype(out_ref.dtype)
    out_ref[:, inner:] = imag.astype(out_ref.dtype)


def link(tile, exponents, mask):
    dates = tile.shape[0]
    inner = TILE * TILE
    outer = SPAN * SPAN
    vmem = pl.BlockSpec(memory_space=VMEM)
    return pl.pallas_call(
        link_kernel,
        out_shape=jax.ShapeDtypeStruct((dates, 2 * inner), BF16),
        in_specs=[vmem] * 4,
        out_specs=vmem,
        scratch_shapes=[
            VMEM((2 * dates * outer // LANES, LANES), F32),
            VMEM((2 * dates, outer), BF16),
            VMEM((outer, 4 * dates), BF16),
            VMEM((2 * dates, outer), BF16),
            VMEM((2, dates, inner), F32),
        ],
        compiler_params=pltpu.CompilerParams(vmem_limit_bytes=LIMIT),
        name="link",
    )(tile, exponents, patch_transform(), mask)


def unpack_kernel(tile_ref, out_ref):
    tile_cols = LANES // TILE
    shape = (8, LANES)
    sub = iota(shape, 0)
    column = iota(shape, 1) // TILE
    halves = TILE // 8
    for tile_row in range(tile_ref.shape[0] // tile_cols):
        for plane in range(2):
            for half in range(halves):
                first = (plane * halves + half) * LANES
                value = tile_ref[
                    tile_row * tile_cols : (tile_row + 1) * tile_cols, first : first + LANES
                ].astype(F32)
                for step in (1, 2, 4):
                    ahead = pltpu.roll(pltpu.roll(value, 8 - step, 0), TILE * step, 1)
                    behind = pltpu.roll(pltpu.roll(value, step, 0), LANES - TILE * step, 1)
                    sub_bit = jnp.bitwise_and(sub, step) != 0
                    col_bit = jnp.bitwise_and(column, step) != 0
                    swapped = jnp.where(sub_bit, behind, ahead)
                    value = jnp.where(sub_bit == col_bit, value, swapped)
                row = tile_row * TILE + half * 8
                out_ref[plane, 0, row : row + 8, :] = value


def unpack(tiles):
    rows = tiles.shape[0] * TILE * TILE // LANES
    vmem = pl.BlockSpec(memory_space=VMEM)
    return pl.pallas_call(
        unpack_kernel,
        out_shape=jax.ShapeDtypeStruct((2, 1, rows, LANES), F32),
        in_specs=[vmem],
        out_specs=vmem,
        compiler_params=pltpu.CompilerParams(vmem_limit_bytes=LIMIT),
        name="unpack",
    )(tiles)


def both_ways(boundaries):
    return [(k, k + 1) for k in boundaries] + [(k + 1, k) for k in boundaries]


def local(images, shifts, fractions, exponents):
    rows = images.shape[2]
    blocks = lax.axis_size("az")
    block = az_block()
    first = lax.slice_in_dim(images, 0, HALO, axis=2)
    last = lax.slice_in_dim(images, rows - HALO, rows, axis=2)
    is_even = lax.rem(block, 2) == 0
    to_odd = jnp.where(is_even, first, last)
    to_even = jnp.where(is_even, last, first)
    odd = lax.ppermute(to_odd, "az", both_ways(range(1, blocks - 1, 2)))
    even = lax.ppermute(to_even, "az", both_ways(range(0, blocks - 1, 2)))
    packed, near, mask, exponent_row, steps, tap_rows = inner_resample(
        shifts, fractions, images, exponents.reshape(1, exponents.shape[0])
    )
    packed = edge_resample(blocks - 1, steps, tap_rows, images, even, odd, packed, near)
    tile = lax.all_to_all(packed, "date", split_axis=0, concat_axis=0, tiled=True)
    filtered = link(tile, exponent_row, mask)
    filtered = filtered.reshape(filtered.shape[0], -1, LANES)
    returned = lax.all_to_all(filtered, "date", split_axis=0, concat_axis=0, tiled=True)
    return unpack(returned.reshape(returned.shape[0], -1))


def solution(mesh):
    return jax.shard_map(
        local,
        mesh=mesh,
        in_specs=(P(None, "date", "az", None), P("date", None), P("date", None), P()),
        out_specs=P(None, "date", "az", None),
        check_vma=False,
    )
```

```python
import math

import jax
import jax.numpy as jnp
import numpy as np
from jax import lax
from jax.experimental import pallas as pl
from jax.experimental.pallas import tpu as pltpu
from jax.sharding import PartitionSpec as P

PATCH = 16
HALF_WIN = 8
WIN = 17
TAPS = 8
FRAC = 16
REACH = 8
ITERS = 3
EPS = 1e-05
DAMP = 1.0

TILE = 16
SPAN = TILE + 2 * HALF_WIN
HALO = REACH + HALF_WIN
LANES = 128
GROUPS = LANES // SPAN
HALF_TILE = TILE * TILE // 2
HALF_SPAN = (TILE // 2 + 2 * HALF_WIN) * SPAN
AREA = float(WIN * WIN)
LIMIT = 24 * 1024 * 1024

VMEM = pltpu.VMEM
SMEM = pltpu.SMEM
F32 = jnp.float32
BF16 = jnp.bfloat16


def tap_table():
    fraction = np.arange(FRAC, dtype=np.float64)[:, None] / FRAC
    position = np.arange(TAPS, dtype=np.float64)[None, :] - (TAPS // 2 - 1) - fraction
    window = 0.5 + 0.5 * np.cos(2.0 * math.pi * position / TAPS)
    return (np.sinc(position) * window).astype(np.float32)


def patch_transform():
    place = np.arange(TILE * TILE)
    rows, cols = place // TILE, place % TILE
    phase = (rows[:, None] * rows[None, :] + cols[:, None] * cols[None, :]) % PATCH
    angle = 2.0 * math.pi * phase / PATCH
    parts = []
    for full in (np.cos(angle) / PATCH, -np.sin(angle) / PATCH):
        high = full.astype(jnp.bfloat16)
        low = (full - high.astype(np.float64)).astype(jnp.bfloat16)
        parts += [high, low]
    return np.stack(parts)


def iota(shape, dim):
    return lax.broadcasted_iota(jnp.int32, shape, dim)


def split(value):
    high = value.astype(BF16)
    return high, (value - high.astype(F32)).astype(BF16)


def dot(a, b):
    return jnp.dot(a, b, preferred_element_type=F32)


def read_taps(shift_ref, fraction_ref, table_ref):
    row_taps = [table_ref[fraction_ref[0, 0], tap] for tap in range(TAPS)]
    col_taps = [table_ref[fraction_ref[0, 1], tap] for tap in range(TAPS)]
    return shift_ref[0, 0], shift_ref[0, 1], row_taps, col_taps


def filter_rows(source, opening, kept, taps):
    along = taps[0] * source(opening, kept)
    for tap in range(1, TAPS):
        along = along + taps[tap] * source(opening + tap, kept)
    return along


def filter_cols(along, shift, taps):
    at = iota(along.shape, 1) + (shift - (TAPS // 2 - 1))
    turn = TAPS // 2 - 1 + LANES - shift
    total = None
    for tap in range(TAPS):
        moved = pltpu.roll(along, lax.rem(turn - tap, LANES), 1)
        here = at + tap
        moved = jnp.where(jnp.logical_and(here >= 0, here < LANES), moved, 0.0)
        total = taps[tap] * moved if tap == 0 else total + taps[tap] * moved
    return total


def pack_tile(strip_piece, tile_col):
    lane = iota((8, LANES), 1)
    group = lane // SPAN
    place = lane % SPAN
    planes = []
    for plane in range(2):
        tile = None
        for part in reversed(range(GROUPS)):
            this = strip_piece((2 * part - tile_col) % (LANES // TILE), plane, part)
            tile = this if tile is None else jnp.where(group == part, this, tile)
        if tile_col == 0:
            tile = jnp.where(place >= HALF_WIN, tile, 0.0)
        if tile_col == LANES // TILE - 1:
            tile = jnp.where(place < HALF_WIN + TILE, tile, 0.0)
        planes.append(tile)
    return jnp.concatenate(planes, axis=0).astype(BF16)


def inner_kernel(
    shift_ref, fraction_ref, table_ref, own_ref, exponent_ref,
    packed_ref, near_ref, mask_ref, exponent_out_ref, step_ref, tap_ref, rolled,
):
    row_shift, col_shift, row_taps, col_taps = read_taps(shift_ref, fraction_ref, table_ref)
    rows = own_ref.shape[2]
    kept = rows - 2 * HALF_WIN
    opening = HALF_WIN - (TAPS // 2 - 1) + row_shift
    tile_cols = LANES // TILE
    for plane in range(2):
        along = filter_rows(
            lambda first, size: own_ref[plane, 0, pl.ds(first, size), :], opening, kept, row_taps
        )
        total = filter_cols(along, col_shift, col_taps)
        for turn in range(tile_cols):
            moved = pltpu.roll(total, HALF_WIN + TILE * turn, 1)
            rolled[turn, plane] = moved
            near_ref[0, turn, plane] = moved[0:HALO]
            near_ref[1, turn, plane] = moved[kept - HALO : kept]
    for tile_row in range(1, rows // TILE - 1):
        first = (tile_row - 1) * TILE
        for tile_col in range(tile_cols):
            packed_ref[tile_row * tile_cols + tile_col] = pack_tile(
                lambda turn, plane, part: rolled[
                    turn, plane, pl.ds(first + part, 8, stride=GROUPS), :
                ],
                tile_col,
            )
    shape = mask_ref.shape
    at = iota(shape, 0)
    pixel = iota(shape, 1)
    row_lag = at // SPAN - pixel // TILE
    col_lag = at % SPAN - pixel % TILE
    row_ok = jnp.logical_and(row_lag >= 0, row_lag < WIN)
    col_ok = jnp.logical_and(col_lag >= 0, col_lag < WIN)
    mask_ref[...] = jnp.where(jnp.logical_and(row_ok, col_ok), 1.0, 0.0).astype(BF16)
    exponent_out_ref[...] = exponent_ref[...]
    step_ref[0:1, :] = jnp.full((1, LANES), row_shift, jnp.int32)
    step_ref[1:2, :] = jnp.full((1, LANES), col_shift, jnp.int32)
    for tap in range(TAPS):
        tap_ref[tap : tap + 1, :] = jnp.full((1, LANES), row_taps[tap], F32)
        tap_ref[TAPS + tap : TAPS + tap + 1, :] = jnp.full((1, LANES), col_taps[tap], F32)


def inner_resample(shifts, fractions, own, exponents):
    rows = own.shape[2]
    tiles = (rows // TILE) * (LANES // TILE)
    kept = rows - 2 * HALF_WIN
    smem = pl.BlockSpec(memory_space=SMEM)
    vmem = pl.BlockSpec(memory_space=VMEM)
    return pl.pallas_call(
        inner_kernel,
        out_shape=(
            jax.ShapeDtypeStruct((tiles, 2 * 8, LANES), BF16),
            jax.ShapeDtypeStruct((2, LANES // TILE, 2, HALO, LANES), F32),
            jax.ShapeDtypeStruct((HALF_SPAN, HALF_TILE), BF16),
            jax.ShapeDtypeStruct(exponents.shape, F32),
            jax.ShapeDtypeStruct((2, LANES), jnp.int32),
            jax.ShapeDtypeStruct((2 * TAPS, LANES), F32),
        ),
        in_specs=[smem] * 3 + [vmem] * 2,
        out_specs=(vmem,) * 6,
        scratch_shapes=[VMEM((LANES // TILE, 2, kept, LANES), F32)],
        compiler_params=pltpu.CompilerParams(vmem_limit_bytes=LIMIT),
        cost_estimate=pl.CostEstimate(flops=2000000, bytes_accessed=2000000, transcendentals=0),
        name="inner_resample",
    )(shifts, fractions, tap_table(), own, exponents)


def az_block():
    return lax.axis_index("az").astype(jnp.int32)


def edge_kernel(
    below, last_block, step_ref, tap_ref, own_ref, one_ref, two_ref, three_ref, down_ref,
    packed_in_ref, near_ref,
    packed_ref, strip, extended,
):
    rows = own_ref.shape[2]
    row_shift, col_shift = jnp.max(step_ref[0:1, :]), jnp.max(step_ref[1:2, :])
    row_taps = [tap_ref[tap : tap + 1, :] for tap in range(TAPS)]
    col_taps = [tap_ref[TAPS + tap : TAPS + tap + 1, :] for tap in range(TAPS)]
    block = az_block()
    chosen = [
        [jnp.bitwise_and(jnp.right_shift(jnp.int32(bits << shift), block), 1) == 1 for bits in below]
        for shift in (1, 0)
    ]
    tile_cols = LANES // TILE
    tile_rows = rows // TILE
    opening = HALO - HALF_WIN - (TAPS // 2 - 1) + row_shift
    packed_ref[tile_cols : (tile_rows - 1) * tile_cols] = packed_in_ref[
        tile_cols : (tile_rows - 1) * tile_cols
    ]
    for side in range(2):
        row_at = iota((HALO, LANES), 0)
        if side == 0:
            inside = jnp.logical_or(block > 0, row_at >= HALF_WIN)
        else:
            inside = jnp.logical_or(block < last_block, row_at < HALF_WIN)
        for plane in range(2):
            from_near = jnp.zeros((HALO, LANES), F32)
            for take, near_by in zip(chosen[side], (one_ref, two_ref, three_ref)):
                from_near = jnp.where(take, near_by[plane, 0], from_near)
            if side == 0:
                extended[side, plane, 0:HALO] = from_near
                extended[side, plane, HALO : 2 * HALO] = own_ref[plane, 0, 0:HALO]
            else:
                extended[side, plane, 0:HALO] = own_ref[plane, 0, rows - HALO : rows]
                extended[side, plane, HALO : 2 * HALO] = from_near + down_ref[plane, 0]
            along = filter_rows(
                lambda first, size: extended[side, plane, pl.ds(first, size), :],
                opening, HALO, row_taps,
            )
            total = jnp.where(inside, filter_cols(along, col_shift, col_taps), 0.0)
            for turn in range(tile_cols):
                strip[side, turn, plane, side * HALO : (side + 1) * HALO] = pltpu.roll(
                    total, HALF_WIN + TILE * turn, 1
                )
                strip[side, turn, plane, (1 - side) * HALO : (2 - side) * HALO] = near_ref[
                    side, turn, plane
                ]
        tile_row = side * (tile_rows - 1)
        for tile_col in range(tile_cols):
            packed_ref[tile_row * tile_cols + tile_col] = pack_tile(
                lambda turn, plane, part: strip[
                    side, turn, plane, pl.ds(part, 8, stride=GROUPS), :
                ],
                tile_col,
            )


def edge_resample(below, last_block, steps, taps, own, moved, packed, near):
    vmem = pl.BlockSpec(memory_space=VMEM)
    return pl.pallas_call(
        lambda *refs: edge_kernel(below, last_block, *refs),
        out_shape=jax.ShapeDtypeStruct(packed.shape, packed.dtype),
        in_specs=[vmem] * 9,
        out_specs=vmem,
        scratch_shapes=[
            VMEM((2, LANES // TILE, 2, 2 * HALO, LANES), F32),
            VMEM((2, 2, 2 * HALO, LANES), F32),
        ],
        compiler_params=pltpu.CompilerParams(vmem_limit_bytes=LIMIT),
        name="edge_resample",
    )(steps, taps, own, *moved, packed, near)


def link_kernel(
    tile_ref, exponent_ref, transform_ref, mask, out_ref,
    loose, planes, pixels, power, vector,
):
    dates = tile_ref.shape[0]
    count = 2 * dates
    inner = TILE * TILE
    blocks = SPAN * SPAN // LANES
    loose[...] = tile_ref[...].astype(F32).reshape(loose.shape)
    for b in range(blocks):
        here = slice(b * LANES, (b + 1) * LANES)
        real = loose[pl.ds(b, dates, stride=2 * blocks), :]
        imag = loose[pl.ds(blocks + b, dates, stride=2 * blocks), :]
        both = jnp.concatenate([real, imag], axis=0)
        planes[:, here] = both.astype(BF16)
        turned = both.T.astype(BF16)
        pixels[here, 0:count] = turned
        pixels[here, count : 2 * count] = turned
        high, low = split(real * real + imag * imag)
        power[0:dates, here] = high
        power[dates:count, here] = low
    starts = [half * (SPAN * TILE // 2) for half in range(2)]
    keep = mask[...]
    sums = jnp.concatenate([dot(power[:, first : first + HALF_SPAN], keep) for first in starts], axis=1)
    scaling = lax.rsqrt((sums[:dates] + sums[dates:]) / AREA + EPS)
    vector[0] = jnp.ones((dates, inner), F32)
    vector[1] = jnp.zeros((dates, inner), F32)

    def iterate(_, carry):
        for half in range(2):
            cols = slice(half * HALF_TILE, (half + 1) * HALF_TILE)
            real, imag = vector[0, :, cols], vector[1, :, cols]
            scale = scaling[:, cols]
            rh, rl = split(scale * real)
            ih, il = split(scale * imag)
            top = [jnp.concatenate(pair, axis=1) for pair in ((rh, ih), (ih, -rh), (rl, il), (il, -rl))]
            weights = jnp.concatenate(top, axis=0)
            total = jnp.zeros((count, 2 * HALF_TILE), F32)
            step = 256
            for first in range(0, HALF_SPAN, step):
                here = slice(starts[half] + first, starts[half] + first + step)
                near = mask[first : first + step, :].astype(F32)
                products = dot(pixels[here, :], weights)
                kept = (products * jnp.concatenate([near, near], axis=1)).astype(BF16)
                total = total + dot(planes[:, here], kept)
            factor = scale / AREA
            left, right = slice(0, HALF_TILE), slice(HALF_TILE, 2 * HALF_TILE)
            new_real = factor * (total[:dates, left] - total[dates:, right]) + DAMP * real
            new_imag = factor * (total[:dates, right] + total[dates:, left]) + DAMP * imag
            square = jnp.sum(new_real * new_real + new_imag * new_imag, axis=0, keepdims=True)
            inverse = lax.rsqrt(square / dates + EPS)
            vector[0, :, cols] = new_real * inverse
            vector[1, :, cols] = new_imag * inverse
        return carry

    lax.fori_loop(0, ITERS, iterate, 0)

    def transform(real, imag, sign):
        high, low = split(jnp.concatenate([real, imag], axis=0))
        stacked = jnp.concatenate([high, low], axis=0)
        cos = dot(stacked, transform_ref[0]) + dot(stacked, transform_ref[1])
        sin = dot(stacked, transform_ref[2]) + dot(stacked, transform_ref[3])
        cos = cos[:count] + cos[count:]
        sin = sign * (sin[:count] + sin[count:])
        return cos[:dates] - sin[dates:], sin[:dates] + cos[dates:]

    spectrum_real, spectrum_imag = transform(vector[0], vector[1], 1.0)
    square_shape = (dates, dates)
    own = jnp.where(iota(square_shape, 0) == iota(square_shape, 1), exponent_ref[...], 0.0)
    exponent = jnp.sum(own, axis=1, keepdims=True)
    size = spectrum_real * spectrum_real + spectrum_imag * spectrum_imag
    weighting = jnp.exp(exponent * jnp.log1p(size))
    real, imag = transform(spectrum_real * weighting, spectrum_imag * weighting, -1.0)
    out_ref[:, 0:inner] = real.astype(out_ref.dtype)
    out_ref[:, inner:] = imag.astype(out_ref.dtype)


def link(tile, exponents, mask):
    dates = tile.shape[0]
    inner = TILE * TILE
    outer = SPAN * SPAN
    vmem = pl.BlockSpec(memory_space=VMEM)
    return pl.pallas_call(
        link_kernel,
        out_shape=jax.ShapeDtypeStruct((dates, 2 * inner), BF16),
        in_specs=[vmem] * 4,
        out_specs=vmem,
        scratch_shapes=[
            VMEM((2 * dates * outer // LANES, LANES), F32),
            VMEM((2 * dates, outer), BF16),
            VMEM((outer, 4 * dates), BF16),
            VMEM((2 * dates, outer), BF16),
            VMEM((2, dates, inner), F32),
        ],
        compiler_params=pltpu.CompilerParams(vmem_limit_bytes=LIMIT),
        name="link",
    )(tile, exponents, patch_transform(), mask)


def unpack_kernel(tile_ref, out_ref):
    tile_cols = LANES // TILE
    shape = (8, LANES)
    sub = iota(shape, 0)
    column = iota(shape, 1) // TILE
    halves = TILE // 8
    for tile_row in range(tile_ref.shape[0] // tile_cols):
        for plane in range(2):
            for half in range(halves):
                first = (plane * halves + half) * LANES
                value = tile_ref[
                    tile_row * tile_cols : (tile_row + 1) * tile_cols, first : first + LANES
                ].astype(F32)
                for step in (1, 2, 4):
                    ahead = pltpu.roll(pltpu.roll(value, 8 - step, 0), TILE * step, 1)
                    behind = pltpu.roll(pltpu.roll(value, step, 0), LANES - TILE * step, 1)
                    sub_bit = jnp.bitwise_and(sub, step) != 0
                    col_bit = jnp.bitwise_and(column, step) != 0
                    swapped = jnp.where(sub_bit, behind, ahead)
                    value = jnp.where(sub_bit == col_bit, value, swapped)
                row = tile_row * TILE + half * 8
                out_ref[plane, 0, row : row + 8, :] = value


def unpack(tiles):
    rows = tiles.shape[0] * TILE * TILE // LANES
    vmem = pl.BlockSpec(memory_space=VMEM)
    return pl.pallas_call(
        unpack_kernel,
        out_shape=jax.ShapeDtypeStruct((2, 1, rows, LANES), F32),
        in_specs=[vmem],
        out_specs=vmem,
        compiler_params=pltpu.CompilerParams(vmem_limit_bytes=LIMIT),
        name="unpack",
    )(tiles)


def both_ways(boundaries, dates, blocks):
    pairs = [(k, k + 1) for k in boundaries] + [(k + 1, k) for k in boundaries]
    return [(d * blocks + i, d * blocks + j) for d in dates for i, j in pairs]


def after(value, *earlier):
    return lax.optimization_barrier((value, *earlier))[0]


def local(images, shifts, fractions, exponents):
    rows = images.shape[2]
    blocks = lax.axis_size("az")
    dates = lax.axis_size("date")
    middle = blocks // 2 - 1
    block = az_block()
    first = lax.slice_in_dim(images, 0, HALO, axis=2)
    last = lax.slice_in_dim(images, rows - HALO, rows, axis=2)
    late = range(dates // 2, dates)

    def move(value, pairs):
        return lax.ppermute(value, ("date", "az"), pairs)

    def edge(boundaries):
        lower = sum(1 << k for k in boundaries)
        sends_last = jnp.bitwise_and(jnp.right_shift(jnp.int32(lower), block), 1) == 1
        return jnp.where(sends_last, last, first)

    sets = ([k for k in range(blocks - 1) if k != middle and (k + (k > middle)) % 2 == 0],
            [k for k in range(blocks - 1) if k == middle or (k < middle and k % 2 == 1)],
            [k for k in range(middle + 1, blocks - 1) if (k + 1) % 2 == 1])
    half = dates // 2
    relay = move(first, [(d * blocks + middle + 1, (d - half) * blocks) for d in late])
    down = move(relay, [((d - half) * blocks, d * blocks + middle) for d in late])
    one = move(after(edge(sets[0]), relay), both_ways(sets[0], range(dates), blocks))
    pairs = both_ways(sets[1], range(dates), blocks)
    skipped = {(d * blocks + middle + 1, d * blocks + middle) for d in late}
    two = move(after(edge(sets[1]), relay), [p for p in pairs if p not in skipped])
    three = move(after(edge(sets[2]), relay), both_ways(sets[2], range(dates), blocks))
    below = [sum(1 << k for k in chosen) for chosen in sets]
    packed, near, mask, exponent_row, steps, tap_rows = inner_resample(
        shifts, fractions, images, exponents.reshape(1, exponents.shape[0])
    )
    packed = edge_resample(
        below, blocks - 1, steps, tap_rows, images, (one, two, three, down), packed, near
    )
    tile = lax.all_to_all(packed, "date", split_axis=0, concat_axis=0, tiled=True)
    filtered = link(tile, exponent_row, mask)
    filtered = filtered.reshape(filtered.shape[0], -1, LANES)
    returned = lax.all_to_all(filtered, "date", split_axis=0, concat_axis=0, tiled=True)
    return unpack(returned.reshape(returned.shape[0], -1))


def solution(mesh):
    return jax.shard_map(
        local,
        mesh=mesh,
        in_specs=(P(None, "date", "az", None), P("date", None), P("date", None), P()),
        out_specs=P(None, "date", "az", None),
        check_vma=False,
    )
```

```python
import math

import jax
import jax.numpy as jnp
import numpy as np
from jax import lax
from jax.experimental import pallas as pl
from jax.experimental.pallas import tpu as pltpu
from jax.sharding import PartitionSpec as P

PATCH = 16
HALF_WIN = 8
WIN = 17
TAPS = 8
FRAC = 16
REACH = 8
ITERS = 3
EPS = 1e-05
DAMP = 1.0

TILE = 16
SPAN = TILE + 2 * HALF_WIN
HALO = REACH + HALF_WIN
LANES = 128
GROUPS = LANES // SPAN
HALF_TILE = TILE * TILE // 2
HALF_SPAN = (TILE // 2 + 2 * HALF_WIN) * SPAN
AREA = float(WIN * WIN)
LIMIT = 24 * 1024 * 1024

VMEM = pltpu.VMEM
F32 = jnp.float32
BF16 = jnp.bfloat16


def tap_table():
    fraction = np.arange(FRAC, dtype=np.float64)[:, None] / FRAC
    position = np.arange(TAPS, dtype=np.float64)[None, :] - (TAPS // 2 - 1) - fraction
    window = 0.5 + 0.5 * np.cos(2.0 * math.pi * position / TAPS)
    return (np.sinc(position) * window).astype(np.float32)


def patch_transform():
    place = np.arange(TILE * TILE)
    rows, cols = place // TILE, place % TILE
    phase = (rows[:, None] * rows[None, :] + cols[:, None] * cols[None, :]) % PATCH
    angle = 2.0 * math.pi * phase / PATCH
    parts = []
    for full in (np.cos(angle) / PATCH, -np.sin(angle) / PATCH):
        high = full.astype(jnp.bfloat16)
        low = (full - high.astype(np.float64)).astype(jnp.bfloat16)
        parts += [high, low]
    return np.stack(parts)


def iota(shape, dim):
    return lax.broadcasted_iota(jnp.int32, shape, dim)


def split(value):
    high = value.astype(BF16)
    return high, (value - high.astype(F32)).astype(BF16)


def dot(a, b):
    return jnp.dot(a, b, preferred_element_type=F32)


def pick(values, bits):
    if not bits:
        return values[0]
    return jnp.where(bits[0], pick(values[1::2], bits[1:]), pick(values[0::2], bits[1:]))


def lane_value(ref, lane):
    row = ref[...]
    return jnp.max(jnp.where(iota(row.shape, 1) == lane, row, -TAPS * FRAC))


def taps_of(ref, lane):
    table = tap_table()
    fraction = jnp.broadcast_to(ref[:, lane : lane + 1], (1, LANES))
    bits = [jnp.bitwise_and(jnp.right_shift(fraction, k), 1) == 1 for k in range(4)]
    return [pick([float(value) for value in table[:, tap]], bits) for tap in range(TAPS)]


def filter_rows(source, opening, kept, taps):
    along = taps[0] * source(opening, kept)
    for tap in range(1, TAPS):
        along = along + taps[tap] * source(opening + tap, kept)
    return along


def filter_cols(along, shift, taps):
    at = iota(along.shape, 1) + (shift - (TAPS // 2 - 1))
    turn = TAPS // 2 - 1 + LANES - shift
    total = None
    for tap in range(TAPS):
        moved = pltpu.roll(along, lax.rem(turn - tap, LANES), 1)
        here = at + tap
        moved = jnp.where(jnp.logical_and(here >= 0, here < LANES), moved, 0.0)
        total = taps[tap] * moved if tap == 0 else total + taps[tap] * moved
    return total


def pack_tile(strip_piece, tile_col):
    lane = iota((8, LANES), 1)
    group = lane // SPAN
    place = lane % SPAN
    planes = []
    for plane in range(2):
        tile = None
        for part in reversed(range(GROUPS)):
            this = strip_piece((2 * part - tile_col) % (LANES // TILE), plane, part)
            tile = this if tile is None else jnp.where(group == part, this, tile)
        if tile_col == 0:
            tile = jnp.where(place >= HALF_WIN, tile, 0.0)
        if tile_col == LANES // TILE - 1:
            tile = jnp.where(place < HALF_WIN + TILE, tile, 0.0)
        planes.append(tile)
    return jnp.concatenate(planes, axis=0).astype(BF16)


def inner_kernel(
    shift_ref, fraction_ref, own_ref, exponent_ref,
    packed_ref, near_ref, mask_ref, exponent_out_ref, step_ref, tap_ref, rolled,
):
    row_shift, col_shift = lane_value(shift_ref, 0), lane_value(shift_ref, 1)
    row_taps, col_taps = (taps_of(fraction_ref, lane) for lane in range(2))
    rows = own_ref.shape[2]
    kept = rows - 2 * HALF_WIN
    opening = HALF_WIN - (TAPS // 2 - 1) + row_shift
    tile_cols = LANES // TILE
    for plane in range(2):
        along = filter_rows(
            lambda first, size: own_ref[plane, 0, pl.ds(first, size), :], opening, kept, row_taps
        )
        total = filter_cols(along, col_shift, col_taps)
        for turn in range(tile_cols):
            moved = pltpu.roll(total, HALF_WIN + TILE * turn, 1)
            rolled[turn, plane] = moved
            near_ref[0, turn, plane] = moved[0:HALO]
            near_ref[1, turn, plane] = moved[kept - HALO : kept]
    for tile_row in range(1, rows // TILE - 1):
        first = (tile_row - 1) * TILE
        for tile_col in range(tile_cols):
            packed_ref[tile_row * tile_cols + tile_col] = pack_tile(
                lambda turn, plane, part: rolled[
                    turn, plane, pl.ds(first + part, 8, stride=GROUPS), :
                ],
                tile_col,
            )
    shape = mask_ref.shape
    at = iota(shape, 0)
    pixel = iota(shape, 1)
    row_lag = at // SPAN - pixel // TILE
    col_lag = at % SPAN - pixel % TILE
    row_ok = jnp.logical_and(row_lag >= 0, row_lag < WIN)
    col_ok = jnp.logical_and(col_lag >= 0, col_lag < WIN)
    mask_ref[...] = jnp.where(jnp.logical_and(row_ok, col_ok), 1.0, 0.0).astype(BF16)
    exponent_out_ref[...] = exponent_ref[...]
    step_ref[0:1, :] = jnp.full((1, LANES), row_shift, jnp.int32)
    step_ref[1:2, :] = jnp.full((1, LANES), col_shift, jnp.int32)
    for tap in range(TAPS):
        tap_ref[tap : tap + 1, :] = row_taps[tap]
        tap_ref[TAPS + tap : TAPS + tap + 1, :] = col_taps[tap]


def inner_resample(shifts, fractions, own, exponents):
    rows = own.shape[2]
    tiles = (rows // TILE) * (LANES // TILE)
    kept = rows - 2 * HALF_WIN
    vmem = pl.BlockSpec(memory_space=VMEM)
    return pl.pallas_call(
        inner_kernel,
        out_shape=(
            jax.ShapeDtypeStruct((tiles, 2 * 8, LANES), BF16),
            jax.ShapeDtypeStruct((2, LANES // TILE, 2, HALO, LANES), F32),
            jax.ShapeDtypeStruct((HALF_SPAN, HALF_TILE), BF16),
            jax.ShapeDtypeStruct(exponents.shape, F32),
            jax.ShapeDtypeStruct((2, LANES), jnp.int32),
            jax.ShapeDtypeStruct((2 * TAPS, LANES), F32),
        ),
        in_specs=[vmem] * 4,
        out_specs=(vmem,) * 6,
        scratch_shapes=[VMEM((LANES // TILE, 2, kept, LANES), F32)],
        compiler_params=pltpu.CompilerParams(vmem_limit_bytes=LIMIT),
        cost_estimate=pl.CostEstimate(flops=2000000, bytes_accessed=2000000, transcendentals=0),
        name="inner_resample",
    )(shifts, fractions, own, exponents)


def az_block():
    return lax.axis_index("az").astype(jnp.int32)


def edge_kernel(
    below, last_block, step_ref, tap_ref, own_ref, one_ref, two_ref, three_ref, down_ref,
    packed_in_ref, near_ref,
    packed_ref, strip, extended,
):
    rows = own_ref.shape[2]
    row_shift, col_shift = jnp.max(step_ref[0:1, :]), jnp.max(step_ref[1:2, :])
    row_taps = [tap_ref[tap : tap + 1, :] for tap in range(TAPS)]
    col_taps = [tap_ref[TAPS + tap : TAPS + tap + 1, :] for tap in range(TAPS)]
    block = az_block()
    chosen = [
        [jnp.bitwise_and(jnp.right_shift(jnp.int32(bits << shift), block), 1) == 1 for bits in below]
        for shift in (1, 0)
    ]
    tile_cols = LANES // TILE
    tile_rows = rows // TILE
    opening = HALO - HALF_WIN - (TAPS // 2 - 1) + row_shift
    packed_ref[tile_cols : (tile_rows - 1) * tile_cols] = packed_in_ref[
        tile_cols : (tile_rows - 1) * tile_cols
    ]
    for side in range(2):
        row_at = iota((HALO, LANES), 0)
        if side == 0:
            inside = jnp.logical_or(block > 0, row_at >= HALF_WIN)
        else:
            inside = jnp.logical_or(block < last_block, row_at < HALF_WIN)
        for plane in range(2):
            from_near = jnp.zeros((HALO, LANES), F32)
            for take, near_by in zip(chosen[side], (one_ref, two_ref, three_ref)):
                from_near = jnp.where(take, near_by[plane, 0], from_near)
            if side == 0:
                extended[side, plane, 0:HALO] = from_near
                extended[side, plane, HALO : 2 * HALO] = own_ref[plane, 0, 0:HALO]
            else:
                extended[side, plane, 0:HALO] = own_ref[plane, 0, rows - HALO : rows]
                extended[side, plane, HALO : 2 * HALO] = from_near + down_ref[plane, 0]
            along = filter_rows(
                lambda first, size: extended[side, plane, pl.ds(first, size), :],
                opening, HALO, row_taps,
            )
            total = jnp.where(inside, filter_cols(along, col_shift, col_taps), 0.0)
            for turn in range(tile_cols):
                strip[side, turn, plane, side * HALO : (side + 1) * HALO] = pltpu.roll(
                    total, HALF_WIN + TILE * turn, 1
                )
                strip[side, turn, plane, (1 - side) * HALO : (2 - side) * HALO] = near_ref[
                    side, turn, plane
                ]
        tile_row = side * (tile_rows - 1)
        for tile_col in range(tile_cols):
            packed_ref[tile_row * tile_cols + tile_col] = pack_tile(
                lambda turn, plane, part: strip[
                    side, turn, plane, pl.ds(part, 8, stride=GROUPS), :
                ],
                tile_col,
            )


def edge_resample(below, last_block, steps, taps, own, moved, packed, near):
    vmem = pl.BlockSpec(memory_space=VMEM)
    return pl.pallas_call(
        lambda *refs: edge_kernel(below, last_block, *refs),
        out_shape=jax.ShapeDtypeStruct(packed.shape, packed.dtype),
        in_specs=[vmem] * 9,
        out_specs=vmem,
        scratch_shapes=[
            VMEM((2, LANES // TILE, 2, 2 * HALO, LANES), F32),
            VMEM((2, 2, 2 * HALO, LANES), F32),
        ],
        compiler_params=pltpu.CompilerParams(vmem_limit_bytes=LIMIT),
        name="edge_resample",
    )(steps, taps, own, *moved, packed, near)


def link_kernel(
    tile_ref, exponent_ref, transform_ref, mask, out_ref,
    loose, planes, pixels, power, vector,
):
    dates = tile_ref.shape[0]
    count = 2 * dates
    inner = TILE * TILE
    blocks = SPAN * SPAN // LANES
    loose[...] = tile_ref[...].astype(F32).reshape(loose.shape)
    for b in range(blocks):
        here = slice(b * LANES, (b + 1) * LANES)
        real = loose[pl.ds(b, dates, stride=2 * blocks), :]
        imag = loose[pl.ds(blocks + b, dates, stride=2 * blocks), :]
        both = jnp.concatenate([real, imag], axis=0)
        planes[:, here] = both.astype(BF16)
        turned = both.T.astype(BF16)
        pixels[here, 0:count] = turned
        pixels[here, count : 2 * count] = turned
        high, low = split(real * real + imag * imag)
        power[0:dates, here] = high
        power[dates:count, here] = low
    starts = [half * (SPAN * TILE // 2) for half in range(2)]
    keep = mask[...]
    sums = jnp.concatenate([dot(power[:, first : first + HALF_SPAN], keep) for first in starts], axis=1)
    scaling = lax.rsqrt((sums[:dates] + sums[dates:]) / AREA + EPS)
    vector[0] = jnp.ones((dates, inner), F32)
    vector[1] = jnp.zeros((dates, inner), F32)

    def iterate(_, norms):
        grown = []
        for half in range(2):
            cols = slice(half * HALF_TILE, (half + 1) * HALF_TILE)
            real, imag = vector[0, :, cols], vector[1, :, cols]
            scale = scaling[:, cols]
            rh, rl = split(scale * real)
            ih, il = split(scale * imag)
            top = [jnp.concatenate(pair, axis=1) for pair in ((rh, ih), (ih, -rh), (rl, il), (il, -rl))]
            weights = jnp.concatenate(top, axis=0)
            total = jnp.zeros((count, 2 * HALF_TILE), F32)
            step = 256
            for first in range(0, HALF_SPAN, step):
                here = slice(starts[half] + first, starts[half] + first + step)
                near = mask[first : first + step, :].astype(F32)
                products = dot(pixels[here, :], weights)
                kept = (products * jnp.concatenate([near, near], axis=1)).astype(BF16)
                total = total + dot(planes[:, here], kept)
            factor = scale / AREA
            left, right = slice(0, HALF_TILE), slice(HALF_TILE, 2 * HALF_TILE)
            new_real = factor * (total[:dates, left] - total[dates:, right]) + DAMP * real
            new_imag = factor * (total[:dates, right] + total[dates:, left]) + DAMP * imag
            square = jnp.sum(new_real * new_real + new_imag * new_imag, axis=0, keepdims=True)
            grown.append(square / dates + EPS * norms[half])
            vector[0, :, cols] = new_real
            vector[1, :, cols] = new_imag
        return tuple(grown)

    norms = lax.fori_loop(0, ITERS, iterate, (jnp.ones((1, HALF_TILE), F32),) * 2)
    inverse = lax.rsqrt(jnp.concatenate(norms, axis=1))

    def transform(real, imag, sign):
        high, low = split(jnp.concatenate([real, imag], axis=0))
        stacked = jnp.concatenate([high, low], axis=0)
        cos, sin = dot(stacked, transform_ref[0]), dot(stacked, transform_ref[2])
        cos = cos[:count] + cos[count:] + dot(high, transform_ref[1])
        sin = sign * (sin[:count] + sin[count:] + dot(high, transform_ref[3]))
        return cos[:dates] - sin[dates:], sin[:dates] + cos[dates:]

    spectrum_real, spectrum_imag = transform(vector[0] * inverse, vector[1] * inverse, 1.0)
    square_shape = (dates, dates)
    own = jnp.where(iota(square_shape, 0) == iota(square_shape, 1), exponent_ref[...], 0.0)
    exponent = jnp.sum(own, axis=1, keepdims=True)
    size = spectrum_real * spectrum_real + spectrum_imag * spectrum_imag
    weighting = jnp.exp(exponent * jnp.log1p(size))
    real, imag = transform(spectrum_real * weighting, spectrum_imag * weighting, -1.0)
    out_ref[:, 0:inner] = real.astype(out_ref.dtype)
    out_ref[:, inner:] = imag.astype(out_ref.dtype)


def link(tile, exponents, mask):
    dates = tile.shape[0]
    inner = TILE * TILE
    outer = SPAN * SPAN
    vmem = pl.BlockSpec(memory_space=VMEM)
    return pl.pallas_call(
        link_kernel,
        out_shape=jax.ShapeDtypeStruct((dates, 2 * inner), BF16),
        in_specs=[vmem] * 4,
        out_specs=vmem,
        scratch_shapes=[
            VMEM((2 * dates * outer // LANES, LANES), F32),
            VMEM((2 * dates, outer), BF16),
            VMEM((outer, 4 * dates), BF16),
            VMEM((2 * dates, outer), BF16),
            VMEM((2, dates, inner), F32),
        ],
        compiler_params=pltpu.CompilerParams(vmem_limit_bytes=LIMIT),
        name="link",
    )(tile, exponents, patch_transform(), mask)


def unpack_kernel(tile_ref, out_ref):
    tile_cols = LANES // TILE
    shape = (8, LANES)
    sub = iota(shape, 0)
    column = iota(shape, 1) // TILE
    halves = TILE // 8
    for tile_row in range(tile_ref.shape[0] // tile_cols):
        for plane in range(2):
            for half in range(halves):
                first = (plane * halves + half) * LANES
                value = tile_ref[
                    tile_row * tile_cols : (tile_row + 1) * tile_cols, first : first + LANES
                ].astype(F32)
                for step in (1, 2, 4):
                    ahead = pltpu.roll(pltpu.roll(value, 8 - step, 0), TILE * step, 1)
                    behind = pltpu.roll(pltpu.roll(value, step, 0), LANES - TILE * step, 1)
                    sub_bit = jnp.bitwise_and(sub, step) != 0
                    col_bit = jnp.bitwise_and(column, step) != 0
                    swapped = jnp.where(sub_bit, behind, ahead)
                    value = jnp.where(sub_bit == col_bit, value, swapped)
                row = tile_row * TILE + half * 8
                out_ref[plane, 0, row : row + 8, :] = value


def unpack(tiles):
    rows = tiles.shape[0] * TILE * TILE // LANES
    vmem = pl.BlockSpec(memory_space=VMEM)
    return pl.pallas_call(
        unpack_kernel,
        out_shape=jax.ShapeDtypeStruct((2, 1, rows, LANES), F32),
        in_specs=[vmem],
        out_specs=vmem,
        compiler_params=pltpu.CompilerParams(vmem_limit_bytes=LIMIT),
        name="unpack",
    )(tiles)


def both_ways(boundaries, dates, blocks):
    pairs = [(k, k + 1) for k in boundaries] + [(k + 1, k) for k in boundaries]
    return [(d * blocks + i, d * blocks + j) for d in dates for i, j in pairs]


def after(value, *earlier):
    return lax.optimization_barrier((value, *earlier))[0]


def local(images, shifts, fractions, exponents):
    rows = images.shape[2]
    blocks = lax.axis_size("az")
    dates = lax.axis_size("date")
    middle = blocks // 2 - 1
    block = az_block()
    first = lax.slice_in_dim(images, 0, HALO, axis=2)
    last = lax.slice_in_dim(images, rows - HALO, rows, axis=2)
    late = range(dates // 2, dates)

    def move(value, pairs):
        return lax.ppermute(value, ("date", "az"), pairs)

    def edge(boundaries):
        lower = sum(1 << k for k in boundaries)
        sends_last = jnp.bitwise_and(jnp.right_shift(jnp.int32(lower), block), 1) == 1
        return jnp.where(sends_last, last, first)

    sets = ([k for k in range(blocks - 1) if k != middle and (k + (k > middle)) % 2 == 0],
            [k for k in range(blocks - 1) if k == middle or (k < middle and k % 2 == 1)],
            [k for k in range(middle + 1, blocks - 1) if (k + 1) % 2 == 1])
    half = dates // 2
    relay = move(first, [(d * blocks + middle + 1, (d - half) * blocks) for d in late])
    down = move(relay, [((d - half) * blocks, d * blocks + middle) for d in late])
    one = move(after(edge(sets[0]), relay), both_ways(sets[0], range(dates), blocks))
    pairs = both_ways(sets[1], range(dates), blocks)
    skipped = {(d * blocks + middle + 1, d * blocks + middle) for d in late}
    two = move(after(edge(sets[1]), relay), [p for p in pairs if p not in skipped])
    three = move(after(edge(sets[2]), relay), both_ways(sets[2], range(dates), blocks))
    below = [sum(1 << k for k in chosen) for chosen in sets]
    packed, near, mask, exponent_row, steps, tap_rows = inner_resample(
        shifts, fractions, images, exponents.reshape(1, exponents.shape[0])
    )
    packed = edge_resample(
        below, blocks - 1, steps, tap_rows, images, (one, two, three, down), packed, near
    )
    tile = lax.all_to_all(packed, "date", split_axis=0, concat_axis=0, tiled=True)
    filtered = link(tile, exponent_row, mask)
    filtered = filtered.reshape(filtered.shape[0], -1, LANES)
    returned = lax.all_to_all(filtered, "date", split_axis=0, concat_axis=0, tiled=True)
    return unpack(returned.reshape(returned.shape[0], -1))


def solution(mesh):
    return jax.shard_map(
        local,
        mesh=mesh,
        in_specs=(P(None, "date", "az", None), P("date", None), P("date", None), P()),
        out_specs=P(None, "date", "az", None),
        check_vma=False,
    )
```

```python
import math

import jax
import jax.numpy as jnp
import numpy as np
from jax import lax
from jax.experimental import pallas as pl
from jax.experimental.pallas import tpu as pltpu
from jax.sharding import PartitionSpec as P

PATCH = 16
HALF_WIN = 8
WIN = 17
TAPS = 8
FRAC = 16
REACH = 8
ITERS = 3
EPS = 1e-05
DAMP = 1.0

TILE = 16
SPAN = TILE + 2 * HALF_WIN
HALO = REACH + HALF_WIN
LANES = 128
GROUPS = LANES // SPAN
HALF_TILE = TILE * TILE // 2
HALF_SPAN = (TILE // 2 + 2 * HALF_WIN) * SPAN
AREA = float(WIN * WIN)
LIMIT = 24 * 1024 * 1024

VMEM = pltpu.VMEM
F32 = jnp.float32
BF16 = jnp.bfloat16


def tap_table():
    fraction = np.arange(FRAC, dtype=np.float64)[:, None] / FRAC
    position = np.arange(TAPS, dtype=np.float64)[None, :] - (TAPS // 2 - 1) - fraction
    window = 0.5 + 0.5 * np.cos(2.0 * math.pi * position / TAPS)
    return (np.sinc(position) * window).astype(np.float32)


def patch_transform():
    place = np.arange(TILE * TILE)
    rows, cols = place // TILE, place % TILE
    phase = (rows[:, None] * rows[None, :] + cols[:, None] * cols[None, :]) % PATCH
    angle = 2.0 * math.pi * phase / PATCH
    parts = []
    for full in (np.cos(angle) / PATCH, -np.sin(angle) / PATCH):
        high = full.astype(jnp.bfloat16)
        low = (full - high.astype(np.float64)).astype(jnp.bfloat16)
        parts += [high, low]
    return np.stack(parts)


def iota(shape, dim):
    return lax.broadcasted_iota(jnp.int32, shape, dim)


def split(value):
    high = value.astype(BF16)
    return high, (value - high.astype(F32)).astype(BF16)


def dot(a, b):
    return jnp.dot(a, b, preferred_element_type=F32)


def pick(values, bits):
    if not bits:
        return values[0]
    return jnp.where(bits[0], pick(values[1::2], bits[1:]), pick(values[0::2], bits[1:]))


def lane_value(ref, lane):
    row = ref[...]
    return jnp.max(jnp.where(iota(row.shape, 1) == lane, row, -TAPS * FRAC))


def taps_of(ref, lane):
    table = tap_table()
    fraction = jnp.broadcast_to(ref[:, lane : lane + 1], (1, LANES))
    bits = [jnp.bitwise_and(jnp.right_shift(fraction, k), 1) == 1 for k in range(4)]
    return [pick([float(value) for value in table[:, tap]], bits) for tap in range(TAPS)]


def filter_rows(source, opening, kept, taps):
    along = taps[0] * source(opening, kept)
    for tap in range(1, TAPS):
        along = along + taps[tap] * source(opening + tap, kept)
    return along


def filter_cols(along, shift, taps):
    at = iota(along.shape, 1) + (shift - (TAPS // 2 - 1))
    turn = TAPS // 2 - 1 + LANES - shift
    total = None
    for tap in range(TAPS):
        moved = pltpu.roll(along, lax.rem(turn - tap, LANES), 1)
        here = at + tap
        moved = jnp.where(jnp.logical_and(here >= 0, here < LANES), moved, 0.0)
        total = taps[tap] * moved if tap == 0 else total + taps[tap] * moved
    return total


def pack_tile(strip_piece, tile_col):
    lane = iota((8, LANES), 1)
    group = lane // SPAN
    place = lane % SPAN
    planes = []
    for plane in range(2):
        tile = None
        for part in reversed(range(GROUPS)):
            this = strip_piece((2 * part - tile_col) % (LANES // TILE), plane, part)
            tile = this if tile is None else jnp.where(group == part, this, tile)
        if tile_col == 0:
            tile = jnp.where(place >= HALF_WIN, tile, 0.0)
        if tile_col == LANES // TILE - 1:
            tile = jnp.where(place < HALF_WIN + TILE, tile, 0.0)
        planes.append(tile)
    return jnp.concatenate(planes, axis=0).astype(BF16)


def inner_kernel(
    shift_ref, fraction_ref, own_ref, exponent_ref,
    packed_ref, near_ref, mask_ref, exponent_out_ref, step_ref, tap_ref, rolled,
):
    row_shift, col_shift = lane_value(shift_ref, 0), lane_value(shift_ref, 1)
    row_taps, col_taps = (taps_of(fraction_ref, lane) for lane in range(2))
    rows = own_ref.shape[2]
    kept = rows - 2 * HALF_WIN
    opening = HALF_WIN - (TAPS // 2 - 1) + row_shift
    tile_cols = LANES // TILE
    for plane in range(2):
        along = filter_rows(
            lambda first, size: own_ref[plane, 0, pl.ds(first, size), :], opening, kept, row_taps
        )
        total = filter_cols(along, col_shift, col_taps)
        for turn in range(tile_cols):
            moved = pltpu.roll(total, HALF_WIN + TILE * turn, 1)
            rolled[turn, plane] = moved
            near_ref[0, turn, plane] = moved[0:HALO]
            near_ref[1, turn, plane] = moved[kept - HALO : kept]
    for tile_row in range(1, rows // TILE - 1):
        first = (tile_row - 1) * TILE
        for tile_col in range(tile_cols):
            packed_ref[tile_row * tile_cols + tile_col] = pack_tile(
                lambda turn, plane, part: rolled[
                    turn, plane, pl.ds(first + part, 8, stride=GROUPS), :
                ],
                tile_col,
            )
    shape = mask_ref.shape
    at = iota(shape, 0)
    pixel = iota(shape, 1)
    row_lag = at // SPAN - pixel // TILE
    col_lag = at % SPAN - pixel % TILE
    row_ok = jnp.logical_and(row_lag >= 0, row_lag < WIN)
    col_ok = jnp.logical_and(col_lag >= 0, col_lag < WIN)
    mask_ref[...] = jnp.where(jnp.logical_and(row_ok, col_ok), 1.0, 0.0).astype(BF16)
    exponent_out_ref[...] = exponent_ref[...]
    step_ref[0:1, :] = jnp.full((1, LANES), row_shift, jnp.int32)
    step_ref[1:2, :] = jnp.full((1, LANES), col_shift, jnp.int32)
    for tap in range(TAPS):
        tap_ref[tap : tap + 1, :] = row_taps[tap]
        tap_ref[TAPS + tap : TAPS + tap + 1, :] = col_taps[tap]


def inner_resample(shifts, fractions, own, exponents):
    rows = own.shape[2]
    tiles = (rows // TILE) * (LANES // TILE)
    kept = rows - 2 * HALF_WIN
    vmem = pl.BlockSpec(memory_space=VMEM)
    return pl.pallas_call(
        inner_kernel,
        out_shape=(
            jax.ShapeDtypeStruct((tiles, 2 * 8, LANES), BF16),
            jax.ShapeDtypeStruct((2, LANES // TILE, 2, HALO, LANES), F32),
            jax.ShapeDtypeStruct((HALF_SPAN, HALF_TILE), BF16),
            jax.ShapeDtypeStruct(exponents.shape, F32),
            jax.ShapeDtypeStruct((2, LANES), jnp.int32),
            jax.ShapeDtypeStruct((2 * TAPS, LANES), F32),
        ),
        in_specs=[vmem] * 4,
        out_specs=(vmem,) * 6,
        scratch_shapes=[VMEM((LANES // TILE, 2, kept, LANES), F32)],
        compiler_params=pltpu.CompilerParams(vmem_limit_bytes=LIMIT),
        cost_estimate=pl.CostEstimate(flops=2000000, bytes_accessed=2000000, transcendentals=0),
        name="inner_resample",
    )(shifts, fractions, own, exponents)


def az_block():
    return lax.axis_index("az").astype(jnp.int32)


def edge_kernel(
    below, last_block, step_ref, tap_ref, own_ref, one_ref, two_ref, three_ref, down_ref,
    packed_in_ref, near_ref,
    packed_ref, strip, extended,
):
    rows = own_ref.shape[2]
    row_shift, col_shift = jnp.max(step_ref[0:1, :]), jnp.max(step_ref[1:2, :])
    row_taps = [tap_ref[tap : tap + 1, :] for tap in range(TAPS)]
    col_taps = [tap_ref[TAPS + tap : TAPS + tap + 1, :] for tap in range(TAPS)]
    block = az_block()
    chosen = [
        [jnp.bitwise_and(jnp.right_shift(jnp.int32(bits << shift), block), 1) == 1 for bits in below]
        for shift in (1, 0)
    ]
    tile_cols = LANES // TILE
    tile_rows = rows // TILE
    opening = HALO - HALF_WIN - (TAPS // 2 - 1) + row_shift
    packed_ref[tile_cols : (tile_rows - 1) * tile_cols] = packed_in_ref[
        tile_cols : (tile_rows - 1) * tile_cols
    ]
    for side in range(2):
        row_at = iota((HALO, LANES), 0)
        if side == 0:
            inside = jnp.logical_or(block > 0, row_at >= HALF_WIN)
        else:
            inside = jnp.logical_or(block < last_block, row_at < HALF_WIN)
        for plane in range(2):
            from_near = jnp.zeros((HALO, LANES), F32)
            for take, near_by in zip(chosen[side], (one_ref, two_ref, three_ref)):
                from_near = jnp.where(take, near_by[plane, 0], from_near)
            if side == 0:
                extended[side, plane, 0:HALO] = from_near
                extended[side, plane, HALO : 2 * HALO] = own_ref[plane, 0, 0:HALO]
            else:
                extended[side, plane, 0:HALO] = own_ref[plane, 0, rows - HALO : rows]
                extended[side, plane, HALO : 2 * HALO] = from_near + down_ref[plane, 0]
            along = filter_rows(
                lambda first, size: extended[side, plane, pl.ds(first, size), :],
                opening, HALO, row_taps,
            )
            total = jnp.where(inside, filter_cols(along, col_shift, col_taps), 0.0)
            for turn in range(tile_cols):
                strip[side, turn, plane, side * HALO : (side + 1) * HALO] = pltpu.roll(
                    total, HALF_WIN + TILE * turn, 1
                )
                strip[side, turn, plane, (1 - side) * HALO : (2 - side) * HALO] = near_ref[
                    side, turn, plane
                ]
        tile_row = side * (tile_rows - 1)
        for tile_col in range(tile_cols):
            packed_ref[tile_row * tile_cols + tile_col] = pack_tile(
                lambda turn, plane, part: strip[
                    side, turn, plane, pl.ds(part, 8, stride=GROUPS), :
                ],
                tile_col,
            )


def edge_resample(below, last_block, steps, taps, own, moved, packed, near):
    vmem = pl.BlockSpec(memory_space=VMEM)
    return pl.pallas_call(
        lambda *refs: edge_kernel(below, last_block, *refs),
        out_shape=jax.ShapeDtypeStruct(packed.shape, packed.dtype),
        in_specs=[vmem] * 9,
        out_specs=vmem,
        scratch_shapes=[
            VMEM((2, LANES // TILE, 2, 2 * HALO, LANES), F32),
            VMEM((2, 2, 2 * HALO, LANES), F32),
        ],
        compiler_params=pltpu.CompilerParams(vmem_limit_bytes=LIMIT),
        name="edge_resample",
    )(steps, taps, own, *moved, packed, near)


def link_kernel(
    tile_ref, exponent_ref, transform_ref, mask, out_ref,
    loose, planes, pixels, power, vector,
):
    dates = tile_ref.shape[0]
    count = 2 * dates
    inner = TILE * TILE
    blocks = SPAN * SPAN // LANES
    loose[...] = tile_ref[...].astype(F32).reshape(loose.shape)
    for b in range(blocks):
        here = slice(b * LANES, (b + 1) * LANES)
        real = loose[pl.ds(b, dates, stride=2 * blocks), :]
        imag = loose[pl.ds(blocks + b, dates, stride=2 * blocks), :]
        both = jnp.concatenate([real, imag], axis=0)
        planes[:, here] = both.astype(BF16)
        turned = both.T.astype(BF16)
        pixels[here, 0:count] = turned
        pixels[here, count : 2 * count] = turned
        high, low = split(real * real + imag * imag)
        power[0:dates, here] = high
        power[dates:count, here] = low
    starts = [half * (SPAN * TILE // 2) for half in range(2)]
    keep = mask[...]
    sums = jnp.concatenate([dot(power[:, first : first + HALF_SPAN], keep) for first in starts], axis=1)
    scaling = lax.rsqrt((sums[:dates] + sums[dates:]) / AREA + EPS)
    vector[0] = jnp.ones((dates, inner), F32)
    vector[1] = jnp.zeros((dates, inner), F32)

    def iterate(_, norms):
        grown = []
        for half in range(2):
            cols = slice(half * HALF_TILE, (half + 1) * HALF_TILE)
            real, imag = vector[0, :, cols], vector[1, :, cols]
            scale = scaling[:, cols]
            rh, rl = split(scale * real)
            ih, il = split(scale * imag)
            top = [jnp.concatenate(pair, axis=1) for pair in ((rh, ih), (ih, -rh), (rl, il), (il, -rl))]
            weights = jnp.concatenate(top, axis=0)
            total = jnp.zeros((count, 2 * HALF_TILE), F32)
            step = 256
            for first in range(0, HALF_SPAN, step):
                here = slice(starts[half] + first, starts[half] + first + step)
                near = mask[first : first + step, :].astype(F32)
                products = dot(pixels[here, :], weights)
                kept = (products * jnp.concatenate([near, near], axis=1)).astype(BF16)
                total = total + dot(planes[:, here], kept)
            factor = scale / AREA
            left, right = slice(0, HALF_TILE), slice(HALF_TILE, 2 * HALF_TILE)
            new_real = factor * (total[:dates, left] - total[dates:, right]) + DAMP * real
            new_imag = factor * (total[:dates, right] + total[dates:, left]) + DAMP * imag
            square = jnp.sum(new_real * new_real + new_imag * new_imag, axis=0, keepdims=True)
            grown.append(square / dates + EPS * norms[half])
            vector[0, :, cols] = new_real
            vector[1, :, cols] = new_imag
        return tuple(grown)

    norms = lax.fori_loop(0, ITERS, iterate, (jnp.ones((1, HALF_TILE), F32),) * 2)
    inverse = lax.rsqrt(jnp.concatenate(norms, axis=1))

    def transform(real, imag, sign):
        high, low = split(jnp.concatenate([real, imag], axis=0))
        stacked = jnp.concatenate([high, low], axis=0)
        cos, sin = dot(stacked, transform_ref[0]), dot(stacked, transform_ref[2])
        cos = cos[:count] + cos[count:] + dot(high, transform_ref[1])
        sin = sign * (sin[:count] + sin[count:] + dot(high, transform_ref[3]))
        return cos[:dates] - sin[dates:], sin[:dates] + cos[dates:]

    spectrum_real, spectrum_imag = transform(vector[0] * inverse, vector[1] * inverse, 1.0)
    square_shape = (dates, dates)
    own = jnp.where(iota(square_shape, 0) == iota(square_shape, 1), exponent_ref[...], 0.0)
    exponent = jnp.sum(own, axis=1, keepdims=True)
    size = spectrum_real * spectrum_real + spectrum_imag * spectrum_imag
    weighting = jnp.exp(exponent * jnp.log1p(size))
    real, imag = transform(spectrum_real * weighting, spectrum_imag * weighting, -1.0)
    out_ref[:, 0:inner] = real.astype(out_ref.dtype)
    out_ref[:, inner:] = imag.astype(out_ref.dtype)


def link(tile, exponents, mask):
    dates = tile.shape[0]
    inner = TILE * TILE
    outer = SPAN * SPAN
    vmem = pl.BlockSpec(memory_space=VMEM)
    return pl.pallas_call(
        link_kernel,
        out_shape=jax.ShapeDtypeStruct((dates, 2 * inner), BF16),
        in_specs=[vmem] * 4,
        out_specs=vmem,
        scratch_shapes=[
            VMEM((2 * dates * outer // LANES, LANES), F32),
            VMEM((2 * dates, outer), BF16),
            VMEM((outer, 4 * dates), BF16),
            VMEM((2 * dates, outer), BF16),
            VMEM((2, dates, inner), F32),
        ],
        compiler_params=pltpu.CompilerParams(vmem_limit_bytes=LIMIT),
        name="link",
    )(tile, exponents, patch_transform(), mask)


def unpack_kernel(tile_ref, out_ref, stage, sems):
    tile_cols = LANES // TILE
    shape = (8, LANES)
    sub = iota(shape, 0)
    column = iota(shape, 1) // TILE
    halves = TILE // 8
    copies = []
    for plane in range(2):
        for tile_row in range(tile_ref.shape[0] // tile_cols):
            for half in range(halves):
                first = (plane * halves + half) * LANES
                value = tile_ref[
                    tile_row * tile_cols : (tile_row + 1) * tile_cols, first : first + LANES
                ].astype(F32)
                for step in (1, 2, 4):
                    ahead = pltpu.roll(pltpu.roll(value, 8 - step, 0), TILE * step, 1)
                    behind = pltpu.roll(pltpu.roll(value, step, 0), LANES - TILE * step, 1)
                    sub_bit = jnp.bitwise_and(sub, step) != 0
                    col_bit = jnp.bitwise_and(column, step) != 0
                    swapped = jnp.where(sub_bit, behind, ahead)
                    value = jnp.where(sub_bit == col_bit, value, swapped)
                row = tile_row * TILE + half * 8
                stage[plane, 0, row : row + 8, :] = value
        copies.append(pltpu.make_async_copy(stage.at[plane], out_ref.at[plane], sems.at[plane]))
        copies[-1].start()
    for copy in copies:
        copy.wait()


def unpack(tiles):
    rows = tiles.shape[0] * TILE * TILE // LANES
    shape = (2, 1, rows, LANES)
    return pl.pallas_call(
        unpack_kernel,
        out_shape=jax.ShapeDtypeStruct(shape, F32),
        in_specs=[pl.BlockSpec(memory_space=VMEM)],
        out_specs=pl.BlockSpec(memory_space=pl.ANY),
        scratch_shapes=[VMEM(shape, F32), pltpu.SemaphoreType.DMA((2,))],
        compiler_params=pltpu.CompilerParams(vmem_limit_bytes=LIMIT),
        name="unpack",
    )(tiles)


def both_ways(boundaries, dates, blocks):
    pairs = [(k, k + 1) for k in boundaries] + [(k + 1, k) for k in boundaries]
    return [(d * blocks + i, d * blocks + j) for d in dates for i, j in pairs]


def after(value, *earlier):
    return lax.optimization_barrier((value, *earlier))[0]


def local(images, shifts, fractions, exponents):
    rows = images.shape[2]
    blocks = lax.axis_size("az")
    dates = lax.axis_size("date")
    middle = blocks // 2 - 1
    block = az_block()
    first = lax.slice_in_dim(images, 0, HALO, axis=2)
    last = lax.slice_in_dim(images, rows - HALO, rows, axis=2)
    late = range(dates // 2, dates)

    def move(value, pairs):
        return lax.ppermute(value, ("date", "az"), pairs)

    def edge(boundaries):
        lower = sum(1 << k for k in boundaries)
        sends_last = jnp.bitwise_and(jnp.right_shift(jnp.int32(lower), block), 1) == 1
        return jnp.where(sends_last, last, first)

    sets = ([k for k in range(blocks - 1) if k != middle and (k + (k > middle)) % 2 == 0],
            [k for k in range(blocks - 1) if k == middle or (k < middle and k % 2 == 1)],
            [k for k in range(middle + 1, blocks - 1) if (k + 1) % 2 == 1])
    half = dates // 2
    relay = move(first, [(d * blocks + middle + 1, (d - half) * blocks) for d in late])
    down = move(relay, [((d - half) * blocks, d * blocks + middle) for d in late])
    one = move(after(edge(sets[0]), relay), both_ways(sets[0], range(dates), blocks))
    pairs = both_ways(sets[1], range(dates), blocks)
    skipped = {(d * blocks + middle + 1, d * blocks + middle) for d in late}
    two = move(after(edge(sets[1]), relay), [p for p in pairs if p not in skipped])
    three = move(after(edge(sets[2]), relay), both_ways(sets[2], range(dates), blocks))
    below = [sum(1 << k for k in chosen) for chosen in sets]
    packed, near, mask, exponent_row, steps, tap_rows = inner_resample(
        shifts, fractions, images, exponents.reshape(1, exponents.shape[0])
    )
    packed = edge_resample(
        below, blocks - 1, steps, tap_rows, images, (one, two, three, down), packed, near
    )
    tile = lax.all_to_all(packed, "date", split_axis=0, concat_axis=0, tiled=True)
    filtered = link(tile, exponent_row, mask)
    filtered = filtered.reshape(filtered.shape[0], -1, LANES)
    returned = lax.all_to_all(filtered, "date", split_axis=0, concat_axis=0, tiled=True)
    return unpack(returned.reshape(returned.shape[0], -1))


def solution(mesh):
    return jax.shard_map(
        local,
        mesh=mesh,
        in_specs=(P(None, "date", "az", None), P("date", None), P("date", None), P()),
        out_specs=P(None, "date", "az", None),
        check_vma=False,
    )
```
